512 devices in a mesh: tile: 64 (over y, x, core), view: 8 (over z).
Axes of the slice: x: 4, y: 8, z: 8, core: 2. Of those that a mesh axis runs over, the one named last changes fastest.
Arguments:
- volume: float32 [64, 512, 512], P(None, 'tile'), may hold values from 0.09 to 7.2
- weights: bfloat16 [64, 32, 32, 48, 256], P('tile', 'view'), may hold values from 0 to 0.0546875
- measured: float32 [64, 8, 1, 64, 48], P('tile', 'view'), may hold values from 4 to 40
- crossings: int32 [64, 32, 32, 2], P('tile', 'view'), may hold values from 0 to 15, as said below
- counts: int32 [64, 32], P('tile', 'view'), may hold values from 16 to 32
Outputs:
- updated: float32 [64, 512, 512], P(None, 'tile')
The draws below stay inside these ranges and needn't reach their ends.
Inputs may be any that keep to these rules, and one draw needn't show every extreme that they name: `crossings`: slots follow a parallel-beam geometry: each segment of a strip has one or two live slots, naming the one or two adjacent blocks that its pixels' footprints reach in that view; the live slots of a strip and view come first; a dead slot repeats the first block of its segment.
All inputs are finite; a program needn't handle non-finite values.
Results may differ from the reference program's by a relative error of at most 0.002.
Values may be sent and summed in bfloat16 or wider, within the bound.
A program may use at most 64 MiB of HBM per device.

```python
import math
import jax
import jax.numpy as jnp
from jax import lax

PLANES = 64
TROWS = 8
COLS = 512
SEGC = 32
BIN = 48
UBLK = 16
VIEW_DEV = 4
NSEG = 16
SEGPIX = 256
K = 32
VIEWS = 32
ROWS = 512
OWN = 1
N_TILE = 64
N_VIEW = 8


SCALE_RES = 1024


def view_table():
    cosines = []
    sines = []
    for view in range(VIEWS):
        angle = math.pi * view / VIEWS
        cosines.append(int(math.floor(SCALE_RES * math.cos(angle) + 0.5)))
        sines.append(int(math.floor(SCALE_RES * math.sin(angle) + 0.5)))
    return (jnp.array(cosines, dtype=jnp.int32), jnp.array(sines, dtype=jnp.int32))


def pixel_positions(key):
    cosines, sines = view_table()
    detector = UBLK * BIN
    reach = BIN // 3
    shifts = jax.random.randint(jax.random.fold_in(key, 5), (VIEWS,), -reach, reach + 1, dtype=jnp.int32)
    tile = jnp.arange(N_TILE, dtype=jnp.int32)[:, None, None, None, None]
    segment = jnp.arange(NSEG, dtype=jnp.int32)[None, None, :, None, None]
    row = jnp.arange(TROWS, dtype=jnp.int32)[None, None, None, :, None]
    col_local = jnp.arange(SEGC, dtype=jnp.int32)[None, None, None, None, :]
    column = segment * SEGC + col_local
    global_row = tile * TROWS + row
    cos_v = cosines[None, :, None, None, None]
    sin_v = sines[None, :, None, None, None]
    shift_v = shifts[None, :, None, None, None]
    numer = cos_v * (2 * column + 1 - COLS) + sin_v * (2 * global_row + 1 - ROWS)
    numer = numer + SCALE_RES * (detector + 2 * shift_v) - SCALE_RES
    lower = numer // (2 * SCALE_RES)
    rest = numer - lower * (2 * SCALE_RES)
    return (lower.reshape(N_TILE, VIEWS, NSEG, SEGPIX), rest.reshape(N_TILE, VIEWS, NSEG, SEGPIX))


def slot_layout(key):
    lower, rest = pixel_positions(key)
    first_bin = jnp.min(lower, axis=3) - 1
    last_bin = jnp.max(lower, axis=3) + 2
    base_block = first_bin // BIN
    straddles = (last_bin >= (base_block + 1) * BIN).astype(jnp.int32)
    half = jnp.arange(2, dtype=jnp.int32)[None, None, None, :]
    live = jnp.maximum(1 - half, straddles[..., None])
    block = base_block[..., None] + half * live
    seg_id = jnp.broadcast_to(jnp.arange(NSEG, dtype=jnp.int32)[None, None, :, None], live.shape)
    order_key = jnp.where(live == 1, half * NSEG + seg_id, 2 * NSEG + seg_id).reshape(N_TILE, VIEWS, K)
    order = jnp.argsort(order_key, axis=-1, stable=True)
    block = jnp.take_along_axis(block.reshape(N_TILE, VIEWS, K), order, axis=-1)
    segment = jnp.take_along_axis(seg_id.reshape(N_TILE, VIEWS, K), order, axis=-1)
    alive = jnp.take_along_axis(live.reshape(N_TILE, VIEWS, K), order, axis=-1)
    return (block, segment, alive, lower, rest)


def draw_crossings(key, part):
    block, segment, alive, lower, rest = slot_layout(key)
    return jnp.stack([block, segment], axis=-1).astype(jnp.int32)


def draw_counts(key, part):
    block, segment, alive, lower, rest = slot_layout(key)
    return jnp.sum(alive, axis=-1).astype(jnp.int32)


def draw_weights(key, part):
    block, segment, alive, lower, rest = slot_layout(key)
    value_key = jax.random.fold_in(key, 29)
    bins = jnp.arange(BIN, dtype=jnp.int32)[None, None, :, None]

    def one_tile(items):
        tile, tile_block, tile_segment, tile_lower, tile_rest = items
        index = jnp.broadcast_to(tile_segment[..., None], (VIEWS, K, SEGPIX))
        slot_lower = jnp.take_along_axis(tile_lower, index, axis=1)
        slot_rest = jnp.take_along_axis(tile_rest, index, axis=1)
        offset = tile_block[:, :, None, None] * BIN + bins - slot_lower[:, :, None, :]
        fraction = (slot_rest.astype(jnp.float32) / (2.0 * SCALE_RES))[:, :, None, :]
        base = jnp.where(offset == 0, 1.0 - fraction, 0.0)
        base = base + jnp.where(offset == 1, fraction, 0.0)
        base = base + jnp.where((offset == -1) | (offset == 2), 0.25, 0.0)
        tile_key = jax.random.fold_in(value_key, tile)
        spread = jax.random.uniform(tile_key, (VIEWS, K, BIN, SEGPIX), jnp.float32, 0.5, 1.5)
        return (base * spread * (16.0 / COLS)).astype(jnp.bfloat16)
    return lax.map(one_tile, (jnp.arange(N_TILE, dtype=jnp.int32), block, segment, lower, rest))


def draw_volume(key, part):
    key_rough, key_grain = jax.random.split(jax.random.fold_in(key, 11), 2)
    rough = jnp.exp(jax.random.uniform(key_rough, (PLANES, 1, COLS), jnp.float32, math.log(0.3), math.log(3.0)))
    grain = jnp.exp(jax.random.uniform(key_grain, (PLANES, ROWS, COLS), jnp.float32, math.log(0.6), math.log(1.6)))
    return (rough * grain).astype(jnp.float32)


def block_levels(key, shape, shards, low, high):
    def one(axis_at, shards_of):
        draws = jax.random.uniform(jax.random.fold_in(jax.random.fold_in(key, 6), axis_at), (shards_of,), jnp.float32, low / len(shards), high / len(shards))
        return jnp.repeat(jnp.exp(draws), shape[axis_at] // shards_of).reshape((-1,) + (1,) * (len(shape) - axis_at - 1))

    loudness = one(*shards[0])
    for cut in shards[1:]:
        loudness = loudness * one(*cut)
    return loudness


def setup_inputs(seed: int = 0) -> dict:
    key_of = jax.random.split(jax.random.key(seed), 6)
    volume = draw_volume(jax.random.fold_in(key_of[5], 71), 0)
    weights = draw_weights(jax.random.fold_in(key_of[5], 71), 0)
    measured = jnp.clip(jnp.exp(math.log(40.0) - 2.3025851 * jax.random.uniform(key_of[2], (N_TILE, N_VIEW, OWN, PLANES, BIN), jnp.float32) ** block_levels(key_of[2], (N_TILE, N_VIEW, OWN, PLANES, BIN), ((0, 64), (1, 8)), -0.2, 0.2)), 4.0, 40.0)
    crossings = draw_crossings(jax.random.fold_in(key_of[5], 71), 0)
    counts = draw_counts(jax.random.fold_in(key_of[5], 71), 0)
    return {"volume": volume, "weights": weights, "measured": measured, "crossings": crossings, "counts": counts}


BACKGROUND = 1.0
HUBER_DELTA = 0.1


def huber_penalty(volume):
    padded = jnp.pad(volume, 1)
    centre = padded[1:-1, 1:-1, 1:-1]
    total = jnp.zeros_like(volume)
    for other in (padded[2:, 1:-1, 1:-1], padded[:-2, 1:-1, 1:-1], padded[1:-1, 2:, 1:-1],
                  padded[1:-1, :-2, 1:-1], padded[1:-1, 1:-1, 2:], padded[1:-1, 1:-1, :-2]):
        total = total + jnp.clip(centre - other, -HUBER_DELTA, HUBER_DELTA)
    return total


def reference(volume, weights, measured, crossings, counts):
    high = lax.Precision.HIGHEST
    rounded = volume.astype(jnp.bfloat16)
    rounded = lax.optimization_barrier(rounded).astype(jnp.float32)
    tile_vols = rounded.reshape(PLANES, N_TILE, TROWS, NSEG, SEGC).transpose(1, 0, 3, 2, 4)
    tile_vols = tile_vols.reshape(N_TILE, PLANES, NSEG, SEGPIX)
    alive = (jnp.arange(K, dtype=jnp.int32)[None, None, :] < counts[:, :, None]).astype(jnp.float32)
    view_place = jnp.arange(VIEWS, dtype=jnp.int32) % VIEW_DEV
    global_block = view_place[None, :, None] * UBLK + crossings[..., 0]
    route = (global_block[..., None] == jnp.arange(N_TILE * OWN, dtype=jnp.int32)).astype(jnp.float32)
    route = route * alive[..., None]
    chosen = (crossings[..., 1][..., None] == jnp.arange(NSEG, dtype=jnp.int32)).astype(jnp.float32)

    def forward(projection, items):
        tile_vol, tile_w, tile_route, tile_chosen = items
        slot_vol = jnp.einsum('wkq,pqx->wkpx', tile_chosen, tile_vol, precision=high)
        partial_value = jnp.einsum('wkpx,wknx->wkpn', slot_vol, tile_w.astype(jnp.float32), precision=high)
        return projection + jnp.einsum('wkb,wkpn->wbpn', tile_route, partial_value, precision=high), None

    start = jnp.zeros((VIEWS, N_TILE * OWN, PLANES, BIN), jnp.float32)
    projection, _ = lax.scan(forward, start, (tile_vols, weights, route, chosen))
    projection = projection.reshape(N_VIEW, VIEW_DEV, N_TILE * OWN, PLANES, BIN).sum(axis=1)
    counted = measured.transpose(1, 0, 2, 3, 4).reshape(N_VIEW, N_TILE * OWN, PLANES, BIN)
    ratios = (counted / (projection + BACKGROUND)).astype(jnp.bfloat16)
    ratios = lax.optimization_barrier(ratios).astype(jnp.float32)
    per_view = jnp.repeat(ratios, VIEW_DEV, axis=0)

    def backward(carry, items):
        tile_w, tile_route, tile_chosen, tile_alive = items
        wf = tile_w.astype(jnp.float32)
        picked = jnp.einsum('wkb,wbpn->wkpn', tile_route, per_view, precision=high)
        spread = jnp.einsum('wkpn,wknx->wkpx', picked, wf, precision=high)
        back = jnp.einsum('wkq,wkpx->pqx', tile_chosen, spread, precision=high)
        sens = jnp.einsum('wk,wkq,wknx->qx', tile_alive, tile_chosen, wf, precision=high)
        return carry, (back, sens)

    _, (back_all, sens_all) = lax.scan(backward, jnp.float32(0.0), (weights, route, chosen, alive))
    back_sum = back_all.reshape(N_TILE, PLANES, NSEG, TROWS, SEGC).transpose(1, 0, 3, 2, 4)
    back_sum = back_sum.reshape(PLANES, ROWS, COLS)
    sensitivity = sens_all.reshape(N_TILE, NSEG, TROWS, SEGC).transpose(0, 2, 1, 3).reshape(ROWS, COLS)
    penalty = huber_penalty(volume)
    return volume * back_sum / (sensitivity[None] * (1.0 + penalty))
```

```python
import functools

import jax
import jax.numpy as jnp
from jax import lax
from jax.experimental import pallas as pl
from jax.experimental.pallas import tpu as pltpu
from jax.sharding import PartitionSpec as P

BACKGROUND = 1.0
HUBER_DELTA = 0.1
LANES = 128
UNROLL = 8
MESH = pl.DeviceIdType.MESH
VMEM_LIMIT = 24 * 1024 * 1024


def lane_block(shape, width):
    return lax.broadcasted_iota(jnp.int32, shape, len(shape) - 1) // width


def swap_chunks(parts, width):
    chunks = len(parts)
    which = lane_block(parts[0].shape, width)
    outs = []
    for i in range(chunks):
        out = parts[i]
        for j in range(chunks):
            if j != i:
                moved = pltpu.roll(parts[j], ((j - i) * width) % LANES, 1)
                out = jnp.where(which == j, moved, out)
        outs.append(out)
    return outs


def forward_kernel(dims, cross_ref, counts_ref, vol_ref, w_ref, dense_ref, edges_ref, vol, segs, acc):
    planes, rows, cols, seg_cols, views, slots, blocks_view, bins, pc = dims
    per_group = LANES // seg_cols
    half = bins // 2
    total_blocks = views * blocks_view
    first_plane = lax.axis_index("view") * pc
    base = pl.multiple_of(first_plane * rows, rows)
    for g in range(cols // LANES):
        group = slice(LANES * g, LANES * (g + 1))
        vol[g] = vol_ref[:, group]
        edges_ref[0, :, group] = vol[g, pl.ds(base + rows - 1, pc, stride=rows), :]
        edges_ref[1, :, group] = vol[g, pl.ds(base, pc, stride=rows), :]
        for h in range(rows // per_group):
            parts = [
                vol[g, pl.ds(per_group * h + i, planes, stride=rows), :]
                for i in range(per_group)
            ]
            for j, out in enumerate(swap_chunks(parts, seg_cols)):
                out = out.astype(jnp.bfloat16)
                lanes = slice(LANES * h, LANES * (h + 1))
                segs[per_group * g + j, 0:planes, lanes] = out
                segs[per_group * g + j, planes : 2 * planes, lanes] = out
    acc[...] = jnp.zeros_like(acc)
    low = lax.broadcasted_iota(jnp.int32, (half, LANES), 1) < planes

    for w in range(views):
        count = counts_ref[w]

        def body(step, carry, w=w, count=count):
            packed = []
            for u in range(UNROLL):
                k = step * UNROLL + u
                seg = cross_ref[w * 2 * slots + slots + k]
                part = lax.dot_general(
                    w_ref[w * slots + k],
                    segs[seg],
                    (((1,), (1,)), ((), ())),
                    preferred_element_type=jnp.float32,
                )
                packed.append(jnp.where(low, part[:half], part[half:]))
            for u in range(UNROLL):
                k = step * UNROLL + u
                block = cross_ref[w * 2 * slots + k] + w * blocks_view
                at = jnp.where(k < count, block, total_blocks)
                acc[at] += packed[u]
            return carry

        lax.fori_loop(0, (count + UNROLL - 1) // UNROLL, body, 0)
    dense_ref[...] = acc[0:total_blocks].astype(jnp.bfloat16)


def exchange_kernel(
    n_tile, dense_ref, meas_ref, edges_ref, ratios_ref, halo_ref, recv,
    send_sem, recv_sem, gsend_sem, grecv_sem, hsend_sem, hrecv_sem,
):
    me = lax.axis_index("tile")
    view = lax.axis_index("view")
    planes = meas_ref.shape[1]
    half = meas_ref.shape[0] // 2

    def peer_of(k):
        return lax.rem(me + k, n_tile)

    barrier = pltpu.get_barrier_semaphore()

    def greet(k, carry):
        pl.semaphore_signal(barrier, inc=1, device_id=(peer_of(k), view), device_id_type=MESH)
        return carry

    lax.fori_loop(1, n_tile, greet, 0)
    pl.semaphore_wait(barrier, n_tile - 1)

    def send(k, carry):
        peer = peer_of(k)
        pltpu.make_async_remote_copy(
            src_ref=dense_ref.at[peer],
            dst_ref=recv.at[k],
            send_sem=send_sem,
            recv_sem=recv_sem,
            device_id=(peer, view),
            device_id_type=MESH,
        ).start()
        return carry

    lax.fori_loop(1, n_tile, send, 0)
    halos = []
    for side, step in ((0, 1), (1, n_tile - 1)):
        halos.append(
            pltpu.make_async_remote_copy(
                src_ref=edges_ref.at[side],
                dst_ref=halo_ref.at[side],
                send_sem=hsend_sem.at[side],
                recv_sem=hrecv_sem.at[side],
                device_id=(peer_of(step), view),
                device_id_type=MESH,
            )
        )
        halos[-1].start()
    low = lax.broadcasted_iota(jnp.int32, (half, LANES), 1) < planes
    counted = jnp.concatenate([meas_ref[...], meas_ref[...]], axis=1)
    counted = jnp.where(low, counted[:half], counted[half:])
    own = dense_ref[me].astype(jnp.float32)
    rest = pl.ds(1, n_tile - 1)
    pltpu.make_async_copy(recv.at[rest], recv.at[rest], recv_sem).wait()
    total = own
    for k in range(1, n_tile):
        total = total + recv[k].astype(jnp.float32)
    ratio = (counted / (total + BACKGROUND)).astype(jnp.bfloat16)
    ratios_ref[me] = ratio

    def spread(k, carry):
        pltpu.make_async_remote_copy(
            src_ref=ratios_ref.at[me],
            dst_ref=ratios_ref.at[me],
            send_sem=gsend_sem,
            recv_sem=grecv_sem,
            device_id=(peer_of(k), view),
            device_id_type=MESH,
        ).start()
        return carry

    lax.fori_loop(1, n_tile, spread, 0)
    pltpu.make_async_copy(recv.at[rest], recv.at[rest], grecv_sem).wait()
    pltpu.make_async_copy(recv.at[rest], recv.at[rest], send_sem).wait()
    pltpu.make_async_copy(recv.at[rest], recv.at[rest], gsend_sem).wait()
    for copy in halos:
        copy.wait()


def backward_kernel(dims, cross_ref, counts_ref, ratios_ref, w_ref, back_ref, sens_ref, lhs, acc):
    planes, rows, cols, seg_cols, views, slots, blocks_view, bins, pc = dims
    total_blocks = views * blocks_view
    chunks = planes // pc

    def fill(step, carry):
        for u in range(UNROLL):
            b = step * UNROLL + u
            x = ratios_ref[b].astype(jnp.float32)
            x = jnp.concatenate([x, pltpu.roll(x, planes, 1)], axis=0)
            lhs[b, 0:planes] = jnp.transpose(x)[0:planes].astype(jnp.bfloat16)
            lhs[b, planes:] = jnp.ones((lhs.shape[1] - planes, bins), jnp.bfloat16)
        return carry

    lax.fori_loop(0, total_blocks // UNROLL, fill, 0)
    lhs[total_blocks] = jnp.zeros(lhs.shape[1:], jnp.bfloat16)
    acc[...] = jnp.zeros_like(acc)
    for w in range(views):
        count = counts_ref[w]

        def body(step, carry, w=w, count=count):
            spread = []
            for u in range(UNROLL):
                k = step * UNROLL + u
                block = cross_ref[w * 2 * slots + k] + w * blocks_view
                at = jnp.where(k < count, block, total_blocks)
                spread.append(
                    jnp.dot(lhs[at], w_ref[w * slots + k], preferred_element_type=jnp.float32)
                )
            for u in range(UNROLL):
                seg = cross_ref[w * 2 * slots + slots + step * UNROLL + u]
                acc[seg] += spread[u]
            return carry

        lax.fori_loop(0, (count + UNROLL - 1) // UNROLL, body, 0)
    for q in range(acc.shape[0]):
        for c in range(chunks):
            back_ref[c, q] = acc[q, c * pc : (c + 1) * pc].astype(jnp.bfloat16)
        sens_ref[q : q + 1] = acc[q, planes : planes + 1]


def update_kernel(
    sizes, back_ref, sens_ref, vol_ref, halo_ref, out_ref, rback, rsens, natural,
    send_sem, recv_sem, ssend_sem, srecv_sem, gsend_sem, grecv_sem,
):
    n_tile, n_view, seg_cols = sizes
    tile = lax.axis_index("tile")
    me = lax.axis_index("view")
    planes, rows, cols = vol_ref.shape
    pc = planes // n_view
    per_group = LANES // seg_cols

    def peer_of(k):
        return lax.rem(me + k, n_view)

    barrier = pltpu.get_barrier_semaphore()
    for k in range(1, n_view):
        pl.semaphore_signal(barrier, inc=1, device_id=(tile, peer_of(k)), device_id_type=MESH)
    pl.semaphore_wait(barrier, n_view - 1)
    copies = []
    for k in range(1, n_view):
        for src, dst, ss, rs in (
            (sens_ref, rsens.at[k], ssend_sem.at[k], srecv_sem.at[k]),
            (back_ref.at[peer_of(k)], rback.at[k], send_sem.at[k], recv_sem.at[k]),
        ):
            copies.append(
                pltpu.make_async_remote_copy(
                    src_ref=src, dst_ref=dst, send_sem=ss, recv_sem=rs,
                    device_id=(tile, peer_of(k)), device_id_type=MESH,
                )
            )
            copies[-1].start()
    first = pl.multiple_of(me * pc, pc)
    v = vol_ref[pl.ds(first, pc)]
    before = vol_ref[jnp.maximum(first - 1, 0)]
    before = jnp.where(me > 0, before, 0.0)
    after = vol_ref[jnp.minimum(first + pc, planes - 1)]
    after = jnp.where(me < n_view - 1, after, 0.0)
    row = lax.broadcasted_iota(jnp.int32, (pc, rows, cols), 1)
    col = lax.broadcasted_iota(jnp.int32, (pc, rows, cols), 2)
    above = jnp.where(tile > 0, halo_ref[0], 0.0)[:, None, :]
    below = jnp.where(tile < n_tile - 1, halo_ref[1], 0.0)[:, None, :]

    def term(other):
        return jnp.clip(v - other, -HUBER_DELTA, HUBER_DELTA)

    penalty = term(jnp.concatenate([before[None], v[: pc - 1]], axis=0))
    penalty += term(jnp.concatenate([v[1:], after[None]], axis=0))
    penalty += term(jnp.where(row == 0, above, pltpu.roll(v, 1, 1)))
    penalty += term(jnp.where(row == rows - 1, below, pltpu.roll(v, rows - 1, 1)))
    penalty += term(jnp.where(col == 0, 0.0, pltpu.roll(v, 1, 2)))
    penalty += term(jnp.where(col == cols - 1, 0.0, pltpu.roll(v, cols - 1, 2)))
    scale = v / (1.0 + penalty)

    for copy in copies:
        copy.wait_recv()
    sens = sens_ref[...]
    for k in range(1, n_view):
        sens = sens + rsens[k]
    for g in range(cols // LANES):
        parts = []
        for j in range(per_group):
            q = per_group * g + j
            total = back_ref[me, q].astype(jnp.float32)
            for k in range(1, n_view):
                total = total + rback[k, q].astype(jnp.float32)
            parts.append(total / sens[q : q + 1])
        for h in range(rows // per_group):
            lanes = slice(LANES * h, LANES * (h + 1))
            for i, out in enumerate(swap_chunks([x[:, lanes] for x in parts], seg_cols)):
                natural[g, pl.ds(per_group * h + i, pc, stride=rows), :] = out
    for g in range(cols // LANES):
        lanes = slice(LANES * g, LANES * (g + 1))
        out_ref[pl.ds(first, pc), :, lanes] = scale[:, :, lanes] * natural[g].reshape(
            pc, rows, LANES
        )
    mine = out_ref.at[pl.ds(first, pc)]
    final = []
    for k in range(1, n_view):
        final.append(
            pltpu.make_async_remote_copy(
                src_ref=mine, dst_ref=mine, send_sem=gsend_sem.at[k], recv_sem=grecv_sem.at[k],
                device_id=(tile, peer_of(k)), device_id_type=MESH,
            )
        )
        final[-1].start()
    for copy in copies:
        copy.wait_send()
    for copy in final:
        copy.wait()


def per_device(volume, weights, measured, crossings, counts):
    n_tile = lax.axis_size("tile")
    n_view = lax.axis_size("view")
    planes, rows, cols = volume.shape
    views, slots, bins, seg_pixels = weights.shape[1:]
    seg_cols = seg_pixels // rows
    seg_total = cols // seg_cols
    blocks_view = n_tile // views
    pc = planes // n_view
    half = bins // 2
    total = views * blocks_view
    dims = (planes, rows, cols, seg_cols, views, slots, blocks_view, bins, pc)
    f32, bf16 = jnp.float32, jnp.bfloat16
    vmem = pl.BlockSpec(memory_space=pltpu.VMEM)
    smem = pl.BlockSpec(memory_space=pltpu.SMEM)
    dma = pltpu.SemaphoreType.DMA
    local = pltpu.CompilerParams(vmem_limit_bytes=VMEM_LIMIT)

    def remote(number):
        return pltpu.CompilerParams(
            vmem_limit_bytes=VMEM_LIMIT, collective_id=number, has_side_effects=True
        )

    cross = crossings[0].transpose(0, 2, 1).reshape(views * 2 * slots)
    count = counts[0]
    slot_weights = weights.reshape(views * slots, bins, seg_pixels)
    dense, edges = pl.pallas_call(
        functools.partial(forward_kernel, dims),
        out_shape=(
            jax.ShapeDtypeStruct((total, half, LANES), bf16),
            jax.ShapeDtypeStruct((2, pc, cols), f32),
        ),
        in_specs=[smem, smem, vmem, vmem],
        out_specs=(vmem, vmem),
        scratch_shapes=[
            pltpu.VMEM((cols // LANES, planes * rows, LANES), f32),
            pltpu.VMEM((seg_total, 2 * planes, seg_pixels), bf16),
            pltpu.VMEM((total + 1, half, LANES), f32),
        ],
        compiler_params=local,
        name="forward",
    )(cross, count, volume.reshape(planes * rows, cols), slot_weights)
    ratios, halo = pl.pallas_call(
        functools.partial(exchange_kernel, n_tile),
        out_shape=(
            jax.ShapeDtypeStruct((total, half, LANES), bf16),
            jax.ShapeDtypeStruct((2, pc, cols), f32),
        ),
        in_specs=[vmem, vmem, vmem],
        out_specs=(vmem, vmem),
        scratch_shapes=[
            pltpu.VMEM((n_tile, half, LANES), bf16),
            dma, dma, dma, dma, dma((2,)), dma((2,)),
        ],
        compiler_params=remote(1),
        name="exchange",
    )(dense, measured[0, 0, 0].T, edges)
    back, sens = pl.pallas_call(
        functools.partial(backward_kernel, dims),
        out_shape=(
            jax.ShapeDtypeStruct((n_view, seg_total, pc, seg_pixels), bf16),
            jax.ShapeDtypeStruct((seg_total, seg_pixels), f32),
        ),
        in_specs=[smem, smem, vmem, vmem],
        out_specs=(vmem, vmem),
        scratch_shapes=[
            pltpu.VMEM((total + 1, planes + 8, bins), bf16),
            pltpu.VMEM((seg_total, planes + 8, seg_pixels), f32),
        ],
        compiler_params=local,
        name="backward",
    )(cross, count, ratios, slot_weights)
    return pl.pallas_call(
        functools.partial(update_kernel, (n_tile, n_view, seg_cols)),
        out_shape=jax.ShapeDtypeStruct((planes, rows, cols), f32),
        in_specs=[vmem, vmem, vmem, vmem],
        out_specs=vmem,
        scratch_shapes=[
            pltpu.VMEM((n_view, seg_total, pc, seg_pixels), bf16),
            pltpu.VMEM((n_view, seg_total, seg_pixels), f32),
            pltpu.VMEM((cols // LANES, pc * rows, LANES), f32),
        ]
        + [dma((n_view,))] * 6,
        compiler_params=remote(2),
        name="update",
    )(back, sens, volume, halo)


def solution(mesh):
    in_specs = (
        P(None, "tile", None),
        P("tile", "view", None, None, None),
        P("tile", "view", None, None, None),
        P("tile", "view", None, None),
        P("tile", "view"),
    )
    out_specs = P(None, "tile", None)
    return jax.shard_map(
        per_device, mesh=mesh, in_specs=in_specs, out_specs=out_specs, check_vma=False
    )
```

```python
import functools

import jax
import jax.numpy as jnp
from jax import lax
from jax.experimental import pallas as pl
from jax.experimental.pallas import tpu as pltpu
from jax.sharding import PartitionSpec as P

BACKGROUND = 1.0
HUBER_DELTA = 0.1
LANES = 128
UNROLL = 8
MESH = pl.DeviceIdType.MESH
VMEM_LIMIT = 24 * 1024 * 1024


def lane_block(shape, width):
    return lax.broadcasted_iota(jnp.int32, shape, len(shape) - 1) // width


def swap_chunks(parts, width):
    chunks = len(parts)
    which = lane_block(parts[0].shape, width)
    outs = []
    for i in range(chunks):
        out = parts[i]
        for j in range(chunks):
            if j != i:
                moved = pltpu.roll(parts[j], ((j - i) * width) % LANES, 1)
                out = jnp.where(which == j, moved, out)
        outs.append(out)
    return outs


def forward_kernel(dims, cross_ref, counts_ref, vol_ref, w_ref, dense_ref, edges_ref, vol, segs, acc):
    planes, rows, cols, seg_cols, views, slots, blocks_view, bins, pc = dims
    per_group = LANES // seg_cols
    half = bins // 2
    total_blocks = views * blocks_view
    first_plane = lax.axis_index("view") * pc
    base = pl.multiple_of(first_plane * rows, rows)
    for g in range(cols // LANES):
        group = slice(LANES * g, LANES * (g + 1))
        vol[g] = vol_ref[:, group]
        edges_ref[0, :, group] = vol[g, pl.ds(base + rows - 1, pc, stride=rows), :]
        edges_ref[1, :, group] = vol[g, pl.ds(base, pc, stride=rows), :]
        for h in range(rows // per_group):
            parts = [
                vol[g, pl.ds(per_group * h + i, planes, stride=rows), :]
                for i in range(per_group)
            ]
            for j, out in enumerate(swap_chunks(parts, seg_cols)):
                out = out.astype(jnp.bfloat16)
                lanes = slice(LANES * h, LANES * (h + 1))
                segs[per_group * g + j, 0:planes, lanes] = out
                segs[per_group * g + j, planes : 2 * planes, lanes] = out
    acc[...] = jnp.zeros_like(acc)
    low = lax.broadcasted_iota(jnp.int32, (half, LANES), 1) < planes

    for w in range(views):
        count = counts_ref[w]

        def body(step, carry, w=w, count=count):
            packed = []
            for u in range(UNROLL):
                k = step * UNROLL + u
                seg = cross_ref[w * 2 * slots + slots + k]
                part = lax.dot_general(
                    w_ref[w * slots + k],
                    segs[seg],
                    (((1,), (1,)), ((), ())),
                    preferred_element_type=jnp.float32,
                )
                packed.append(jnp.where(low, part[:half], part[half:]))
            for u in range(UNROLL):
                k = step * UNROLL + u
                block = cross_ref[w * 2 * slots + k] + w * blocks_view
                at = jnp.where(k < count, block, total_blocks)
                acc[at] += packed[u]
            return carry

        lax.fori_loop(0, (count + UNROLL - 1) // UNROLL, body, 0)
    dense_ref[...] = acc[0:total_blocks].astype(jnp.bfloat16)


def exchange_kernel(
    n_tile, dense_ref, meas_ref, edges_ref, ratios_ref, halo_ref, recv,
    send_sem, recv_sem, gsend_sem, grecv_sem, hsend_sem, hrecv_sem,
):
    me = lax.axis_index("tile")
    view = lax.axis_index("view")
    planes = meas_ref.shape[1]
    half = meas_ref.shape[0] // 2

    def peer_of(k):
        return lax.rem(me + k, n_tile)

    barrier = pltpu.get_barrier_semaphore()

    def greet(k, carry):
        pl.semaphore_signal(barrier, inc=1, device_id=(peer_of(k), view), device_id_type=MESH)
        return carry

    lax.fori_loop(1, n_tile, greet, 0)
    pl.semaphore_wait(barrier, n_tile - 1)

    def send(k, carry):
        peer = peer_of(k)
        pltpu.make_async_remote_copy(
            src_ref=dense_ref.at[peer],
            dst_ref=recv.at[k],
            send_sem=send_sem,
            recv_sem=recv_sem,
            device_id=(peer, view),
            device_id_type=MESH,
        ).start()
        return carry

    lax.fori_loop(1, n_tile, send, 0)
    halos = []
    for side, step in ((0, 1), (1, n_tile - 1)):
        halos.append(
            pltpu.make_async_remote_copy(
                src_ref=edges_ref.at[side],
                dst_ref=halo_ref.at[side],
                send_sem=hsend_sem.at[side],
                recv_sem=hrecv_sem.at[side],
                device_id=(peer_of(step), view),
                device_id_type=MESH,
            )
        )
        halos[-1].start()
    low = lax.broadcasted_iota(jnp.int32, (half, LANES), 1) < planes
    counted = jnp.concatenate([meas_ref[...], meas_ref[...]], axis=1)
    counted = jnp.where(low, counted[:half], counted[half:])
    own = dense_ref[me].astype(jnp.float32)
    rest = pl.ds(1, n_tile - 1)
    pltpu.make_async_copy(recv.at[rest], recv.at[rest], recv_sem).wait()
    total = own
    for k in range(1, n_tile):
        total = total + recv[k].astype(jnp.float32)
    ratio = (counted / (total + BACKGROUND)).astype(jnp.bfloat16)
    ratios_ref[me] = ratio

    def spread(k, carry):
        pltpu.make_async_remote_copy(
            src_ref=ratios_ref.at[me],
            dst_ref=ratios_ref.at[me],
            send_sem=gsend_sem,
            recv_sem=grecv_sem,
            device_id=(peer_of(k), view),
            device_id_type=MESH,
        ).start()
        return carry

    lax.fori_loop(1, n_tile, spread, 0)
    pltpu.make_async_copy(recv.at[rest], recv.at[rest], grecv_sem).wait()
    pltpu.make_async_copy(recv.at[rest], recv.at[rest], send_sem).wait()
    pltpu.make_async_copy(recv.at[rest], recv.at[rest], gsend_sem).wait()
    for copy in halos:
        copy.wait()


def backward_kernel(dims, cross_ref, counts_ref, ratios_ref, w_ref, back_ref, sens_ref, lhs, acc):
    planes, rows, cols, seg_cols, views, slots, blocks_view, bins, pc = dims
    total_blocks = views * blocks_view
    chunks = planes // pc

    def fill(step, carry):
        for u in range(UNROLL):
            b = step * UNROLL + u
            x = ratios_ref[b].astype(jnp.float32)
            x = jnp.concatenate([x, pltpu.roll(x, planes, 1)], axis=0)
            lhs[b, 0:planes] = jnp.transpose(x)[0:planes].astype(jnp.bfloat16)
            lhs[b, planes:] = jnp.ones((lhs.shape[1] - planes, bins), jnp.bfloat16)
        return carry

    lax.fori_loop(0, total_blocks // UNROLL, fill, 0)
    lhs[total_blocks] = jnp.zeros(lhs.shape[1:], jnp.bfloat16)
    acc[...] = jnp.zeros_like(acc)
    for w in range(views):
        count = counts_ref[w]

        def body(step, carry, w=w, count=count):
            spread = []
            for u in range(UNROLL):
                k = step * UNROLL + u
                block = cross_ref[w * 2 * slots + k] + w * blocks_view
                at = jnp.where(k < count, block, total_blocks)
                spread.append(
                    jnp.dot(lhs[at], w_ref[w * slots + k], preferred_element_type=jnp.float32)
                )
            for u in range(UNROLL):
                seg = cross_ref[w * 2 * slots + slots + step * UNROLL + u]
                acc[seg] += spread[u]
            return carry

        lax.fori_loop(0, (count + UNROLL - 1) // UNROLL, body, 0)
    for q in range(acc.shape[0]):
        for c in range(chunks):
            back_ref[c, q] = acc[q, c * pc : (c + 1) * pc].astype(jnp.bfloat16)
        sens_ref[q : q + 1] = acc[q, planes : planes + 1]


def update_kernel(
    sizes, back_ref, sens_ref, vol_ref, halo_ref, out_ref, rback, rsens, natural,
    send_sem, recv_sem, ssend_sem, srecv_sem, gsend_sem, grecv_sem,
):
    n_tile, n_view, seg_cols = sizes
    tile = lax.axis_index("tile")
    me = lax.axis_index("view")
    planes, rows, cols = vol_ref.shape
    pc = planes // n_view
    per_group = LANES // seg_cols

    def peer_of(k):
        return lax.rem(me + k, n_view)

    def push(src, dst, send, recv, k):
        copy = pltpu.make_async_remote_copy(
            src_ref=src, dst_ref=dst, send_sem=send, recv_sem=recv,
            device_id=(tile, peer_of(k)), device_id_type=MESH,
        )
        copy.start()
        return copy

    barrier = pltpu.get_barrier_semaphore()
    for k in range(1, n_view):
        pl.semaphore_signal(barrier, inc=1, device_id=(tile, peer_of(k)), device_id_type=MESH)
    pl.semaphore_wait(barrier, n_view - 1)
    groups = cols // LANES
    order = sorted(range(1, n_view), key=lambda k: -min(k, n_view - k))
    sens_copies, copies = [], {}
    for k in order:
        sens_copies.append(push(sens_ref, rsens.at[k], ssend_sem.at[k], srecv_sem.at[k], k))
    for g in range(groups):
        piece = pl.ds(per_group * g, per_group)
        for k in order:
            copies[g, k] = push(
                back_ref.at[peer_of(k), piece], rback.at[k, piece],
                send_sem.at[g, k], recv_sem.at[g, k], k,
            )
    first = pl.multiple_of(me * pc, pc)
    v = vol_ref[pl.ds(first, pc)]
    before = vol_ref[jnp.maximum(first - 1, 0)]
    before = jnp.where(me > 0, before, 0.0)
    after = vol_ref[jnp.minimum(first + pc, planes - 1)]
    after = jnp.where(me < n_view - 1, after, 0.0)
    row = lax.broadcasted_iota(jnp.int32, (pc, rows, cols), 1)
    col = lax.broadcasted_iota(jnp.int32, (pc, rows, cols), 2)
    above = jnp.where(tile > 0, halo_ref[0], 0.0)[:, None, :]
    below = jnp.where(tile < n_tile - 1, halo_ref[1], 0.0)[:, None, :]

    def term(other):
        return jnp.clip(v - other, -HUBER_DELTA, HUBER_DELTA)

    penalty = term(jnp.concatenate([before[None], v[: pc - 1]], axis=0))
    penalty += term(jnp.concatenate([v[1:], after[None]], axis=0))
    penalty += term(jnp.where(row == 0, above, pltpu.roll(v, 1, 1)))
    penalty += term(jnp.where(row == rows - 1, below, pltpu.roll(v, rows - 1, 1)))
    penalty += term(jnp.where(col == 0, 0.0, pltpu.roll(v, 1, 2)))
    penalty += term(jnp.where(col == cols - 1, 0.0, pltpu.roll(v, cols - 1, 2)))
    scale = v / (1.0 + penalty)

    for copy in sens_copies:
        copy.wait_recv()
    sens = sens_ref[...]
    for k in range(1, n_view):
        sens = sens + rsens[k]

    def finish(g):
        for k in order:
            copies[g, k].wait_recv()
        parts = []
        for j in range(per_group):
            q = per_group * g + j
            total = back_ref[me, q].astype(jnp.float32)
            for k in range(1, n_view):
                total = total + rback[k, q].astype(jnp.float32)
            parts.append(total / sens[q : q + 1])
        for h in range(rows // per_group):
            lanes = slice(LANES * h, LANES * (h + 1))
            for i, out in enumerate(swap_chunks([x[:, lanes] for x in parts], seg_cols)):
                natural[g, pl.ds(per_group * h + i, pc, stride=rows), :] = out
        lanes = slice(LANES * g, LANES * (g + 1))
        out_ref[pl.ds(first, pc), :, lanes] = scale[:, :, lanes] * natural[g].reshape(
            pc, rows, LANES
        )

    def piece_of(owner, g):
        return out_ref.at[pl.ds(pl.multiple_of(owner * pc, pc), pc), :, LANES * g : LANES * (g + 1)]

    far = n_view // 2
    relays = {}

    def relay(side, hop, g):
        owner = lax.rem(me + (n_view - hop if side == 0 else hop), n_view)
        piece = piece_of(owner, g)
        relays[side, hop, g] = push(
            piece, piece, gsend_sem.at[side, hop, g], grecv_sem.at[side, hop, g],
            1 if side == 0 else n_view - 1,
        )

    def reach(side, g):
        return far if (side == 0) == (g < groups // 2) else n_view - 1 - far

    for tick in range(groups + far):
        for g in range(groups):
            hop = tick - g
            if hop == 0:
                finish(g)
                for side in (0, 1):
                    relay(side, 0, g)
            elif 1 <= hop <= far:
                for side in (0, 1):
                    if hop <= reach(side, g):
                        relays[side, hop - 1, g].wait_recv()
                        if hop < reach(side, g):
                            relay(side, hop, g)
    for copy in sens_copies:
        copy.wait_send()
    for copy in list(copies.values()) + list(relays.values()):
        copy.wait_send()


def per_device(volume, weights, measured, crossings, counts):
    n_tile = lax.axis_size("tile")
    n_view = lax.axis_size("view")
    planes, rows, cols = volume.shape
    views, slots, bins, seg_pixels = weights.shape[1:]
    seg_cols = seg_pixels // rows
    seg_total = cols // seg_cols
    blocks_view = n_tile // views
    pc = planes // n_view
    half = bins // 2
    total = views * blocks_view
    dims = (planes, rows, cols, seg_cols, views, slots, blocks_view, bins, pc)
    f32, bf16 = jnp.float32, jnp.bfloat16
    vmem = pl.BlockSpec(memory_space=pltpu.VMEM)
    smem = pl.BlockSpec(memory_space=pltpu.SMEM)
    dma = pltpu.SemaphoreType.DMA
    local = pltpu.CompilerParams(vmem_limit_bytes=VMEM_LIMIT)

    def remote(number):
        return pltpu.CompilerParams(
            vmem_limit_bytes=VMEM_LIMIT, collective_id=number, has_side_effects=True
        )

    cross = crossings[0].transpose(0, 2, 1).reshape(views * 2 * slots)
    count = counts[0]
    slot_weights = weights.reshape(views * slots, bins, seg_pixels)
    dense, edges = pl.pallas_call(
        functools.partial(forward_kernel, dims),
        out_shape=(
            jax.ShapeDtypeStruct((total, half, LANES), bf16),
            jax.ShapeDtypeStruct((2, pc, cols), f32),
        ),
        in_specs=[smem, smem, vmem, vmem],
        out_specs=(vmem, vmem),
        scratch_shapes=[
            pltpu.VMEM((cols // LANES, planes * rows, LANES), f32),
            pltpu.VMEM((seg_total, 2 * planes, seg_pixels), bf16),
            pltpu.VMEM((total + 1, half, LANES), f32),
        ],
        compiler_params=local,
        name="forward",
    )(cross, count, volume.reshape(planes * rows, cols), slot_weights)
    ratios, halo = pl.pallas_call(
        functools.partial(exchange_kernel, n_tile),
        out_shape=(
            jax.ShapeDtypeStruct((total, half, LANES), bf16),
            jax.ShapeDtypeStruct((2, pc, cols), f32),
        ),
        in_specs=[vmem, vmem, vmem],
        out_specs=(vmem, vmem),
        scratch_shapes=[
            pltpu.VMEM((n_tile, half, LANES), bf16),
            dma, dma, dma, dma, dma((2,)), dma((2,)),
        ],
        compiler_params=remote(1),
        name="exchange",
    )(dense, measured[0, 0, 0].T, edges)
    back, sens = pl.pallas_call(
        functools.partial(backward_kernel, dims),
        out_shape=(
            jax.ShapeDtypeStruct((n_view, seg_total, pc, seg_pixels), bf16),
            jax.ShapeDtypeStruct((seg_total, seg_pixels), f32),
        ),
        in_specs=[smem, smem, vmem, vmem],
        out_specs=(vmem, vmem),
        scratch_shapes=[
            pltpu.VMEM((total + 1, planes + 8, bins), bf16),
            pltpu.VMEM((seg_total, planes + 8, seg_pixels), f32),
        ],
        compiler_params=local,
        name="backward",
    )(cross, count, ratios, slot_weights)
    return pl.pallas_call(
        functools.partial(update_kernel, (n_tile, n_view, seg_cols)),
        out_shape=jax.ShapeDtypeStruct((planes, rows, cols), f32),
        in_specs=[vmem, vmem, vmem, vmem],
        out_specs=vmem,
        scratch_shapes=[
            pltpu.VMEM((n_view, seg_total, pc, seg_pixels), bf16),
            pltpu.VMEM((n_view, seg_total, seg_pixels), f32),
            pltpu.VMEM((cols // LANES, pc * rows, LANES), f32),
        ]
        + [dma((cols // LANES, n_view))] * 2
        + [dma((n_view,))] * 2
        + [dma((2, n_view // 2, cols // LANES))] * 2,
        compiler_params=remote(2),
        name="update",
    )(back, sens, volume, halo)


def solution(mesh):
    in_specs = (
        P(None, "tile", None),
        P("tile", "view", None, None, None),
        P("tile", "view", None, None, None),
        P("tile", "view", None, None),
        P("tile", "view"),
    )
    out_specs = P(None, "tile", None)
    return jax.shard_map(
        per_device, mesh=mesh, in_specs=in_specs, out_specs=out_specs, check_vma=False
    )
```

```python
import functools

import jax
import jax.numpy as jnp
from jax import lax
from jax.experimental import pallas as pl
from jax.experimental.pallas import tpu as pltpu
from jax.sharding import PartitionSpec as P

BACKGROUND = 1.0
HUBER_DELTA = 0.1
LANES = 128
UNROLL = 8
MESH = pl.DeviceIdType.MESH
VMEM_LIMIT = 24 * 1024 * 1024


def lane_block(shape, width):
    return lax.broadcasted_iota(jnp.int32, shape, len(shape) - 1) // width


def swap_chunks(parts, width):
    chunks = len(parts)
    which = lane_block(parts[0].shape, width)
    outs = []
    for i in range(chunks):
        out = parts[i]
        for j in range(chunks):
            if j != i:
                moved = pltpu.roll(parts[j], ((j - i) * width) % LANES, 1)
                out = jnp.where(which == j, moved, out)
        outs.append(out)
    return outs


def forward_kernel(dims, cross_ref, counts_ref, vol_ref, w_ref, dense_ref, edges_ref, vol, segs, acc):
    planes, rows, cols, seg_cols, views, slots, blocks_view, bins, pc = dims
    per_group = LANES // seg_cols
    half = bins // 2
    total_blocks = views * blocks_view
    first_plane = lax.axis_index("view") * pc
    base = pl.multiple_of(first_plane * rows, rows)
    for g in range(cols // LANES):
        group = slice(LANES * g, LANES * (g + 1))
        vol[g] = vol_ref[:, group]
        edges_ref[0, :, group] = vol[g, pl.ds(base + rows - 1, pc, stride=rows), :]
        edges_ref[1, :, group] = vol[g, pl.ds(base, pc, stride=rows), :]
        for h in range(rows // per_group):
            parts = [
                vol[g, pl.ds(per_group * h + i, planes, stride=rows), :]
                for i in range(per_group)
            ]
            for j, out in enumerate(swap_chunks(parts, seg_cols)):
                out = out.astype(jnp.bfloat16)
                lanes = slice(LANES * h, LANES * (h + 1))
                segs[per_group * g + j, 0:planes, lanes] = out
                segs[per_group * g + j, planes : 2 * planes, lanes] = out
    acc[...] = jnp.zeros_like(acc)
    low = lax.broadcasted_iota(jnp.int32, (half, LANES), 1) < planes

    for w in range(views):
        count = counts_ref[w]

        def body(step, carry, w=w, count=count):
            packed = []
            for u in range(UNROLL):
                k = step * UNROLL + u
                seg = cross_ref[w * 2 * slots + slots + k]
                part = lax.dot_general(
                    w_ref[w * slots + k],
                    segs[seg],
                    (((1,), (1,)), ((), ())),
                    preferred_element_type=jnp.float32,
                )
                packed.append(jnp.where(low, part[:half], part[half:]))
            for u in range(UNROLL):
                k = step * UNROLL + u
                block = cross_ref[w * 2 * slots + k] + w * blocks_view
                at = jnp.where(k < count, block, total_blocks)
                acc[at] += packed[u]
            return carry

        lax.fori_loop(0, (count + UNROLL - 1) // UNROLL, body, 0)
    dense_ref[...] = acc[0:total_blocks].astype(jnp.bfloat16)


def exchange_kernel(
    n_tile, dense_ref, meas_ref, edges_ref, ratios_ref, halo_ref, recv,
    send_sem, recv_sem, gsend_sem, grecv_sem, hsend_sem, hrecv_sem,
):
    me = lax.axis_index("tile")
    view = lax.axis_index("view")
    planes = meas_ref.shape[1]
    half = meas_ref.shape[0] // 2

    def peer_of(k):
        return lax.rem(me + k, n_tile)

    barrier = pltpu.get_barrier_semaphore()

    def greet(k, carry):
        pl.semaphore_signal(barrier, inc=1, device_id=(peer_of(k), view), device_id_type=MESH)
        return carry

    lax.fori_loop(1, n_tile, greet, 0)
    pl.semaphore_wait(barrier, n_tile - 1)

    def send(k, carry):
        peer = peer_of(k)
        pltpu.make_async_remote_copy(
            src_ref=dense_ref.at[peer],
            dst_ref=recv.at[k],
            send_sem=send_sem,
            recv_sem=recv_sem,
            device_id=(peer, view),
            device_id_type=MESH,
        ).start()
        return carry

    lax.fori_loop(1, n_tile, send, 0)
    halos = []
    for side, step in ((0, 1), (1, n_tile - 1)):
        halos.append(
            pltpu.make_async_remote_copy(
                src_ref=edges_ref.at[side],
                dst_ref=halo_ref.at[side],
                send_sem=hsend_sem.at[side],
                recv_sem=hrecv_sem.at[side],
                device_id=(peer_of(step), view),
                device_id_type=MESH,
            )
        )
        halos[-1].start()
    low = lax.broadcasted_iota(jnp.int32, (half, LANES), 1) < planes
    counted = jnp.concatenate([meas_ref[...], meas_ref[...]], axis=1)
    counted = jnp.where(low, counted[:half], counted[half:])
    own = dense_ref[me].astype(jnp.float32)
    rest = pl.ds(1, n_tile - 1)
    pltpu.make_async_copy(recv.at[rest], recv.at[rest], recv_sem).wait()
    total = own
    for k in range(1, n_tile):
        total = total + recv[k].astype(jnp.float32)
    ratio = (counted / (total + BACKGROUND)).astype(jnp.bfloat16)
    ratios_ref[me] = ratio

    def spread(k, carry):
        pltpu.make_async_remote_copy(
            src_ref=ratios_ref.at[me],
            dst_ref=ratios_ref.at[me],
            send_sem=gsend_sem,
            recv_sem=grecv_sem,
            device_id=(peer_of(k), view),
            device_id_type=MESH,
        ).start()
        return carry

    lax.fori_loop(1, n_tile, spread, 0)
    pltpu.make_async_copy(recv.at[rest], recv.at[rest], grecv_sem).wait()
    pltpu.make_async_copy(recv.at[rest], recv.at[rest], send_sem).wait()
    pltpu.make_async_copy(recv.at[rest], recv.at[rest], gsend_sem).wait()
    for copy in halos:
        copy.wait()


def backward_kernel(dims, cross_ref, counts_ref, ratios_ref, w_ref, back_ref, sens_ref, lhs, acc):
    planes, rows, cols, seg_cols, views, slots, blocks_view, bins, pc = dims
    total_blocks = views * blocks_view
    chunks = planes // pc

    def fill(step, carry):
        for u in range(UNROLL):
            b = step * UNROLL + u
            x = ratios_ref[b].astype(jnp.float32)
            x = jnp.concatenate([x, pltpu.roll(x, planes, 1)], axis=0)
            lhs[b, 0:planes] = jnp.transpose(x)[0:planes].astype(jnp.bfloat16)
            lhs[b, planes:] = jnp.ones((lhs.shape[1] - planes, bins), jnp.bfloat16)
        return carry

    lax.fori_loop(0, total_blocks // UNROLL, fill, 0)
    lhs[total_blocks] = jnp.zeros(lhs.shape[1:], jnp.bfloat16)
    acc[...] = jnp.zeros_like(acc)
    for w in range(views):
        count = counts_ref[w]

        def body(step, carry, w=w, count=count):
            spread = []
            for u in range(UNROLL):
                k = step * UNROLL + u
                block = cross_ref[w * 2 * slots + k] + w * blocks_view
                at = jnp.where(k < count, block, total_blocks)
                spread.append(
                    jnp.dot(lhs[at], w_ref[w * slots + k], preferred_element_type=jnp.float32)
                )
            for u in range(UNROLL):
                seg = cross_ref[w * 2 * slots + slots + step * UNROLL + u]
                acc[seg] += spread[u]
            return carry

        lax.fori_loop(0, (count + UNROLL - 1) // UNROLL, body, 0)
    for q in range(acc.shape[0]):
        for c in range(chunks):
            back_ref[c, q] = acc[q, c * pc : (c + 1) * pc].astype(jnp.bfloat16)
        sens_ref[q : q + 1] = acc[q, planes : planes + 1]


def update_kernel(
    sizes, back_ref, sens_ref, vol_ref, halo_ref, out_ref, rback, rsens, natural,
    send_sem, ssend_sem, srecv_sem, gsend_sem, recv_sem, grecv_sem,
):
    n_tile, n_view, seg_cols = sizes
    tile = lax.axis_index("tile")
    me = lax.axis_index("view")
    planes, rows, cols = vol_ref.shape
    pc = planes // n_view
    per_group = LANES // seg_cols

    def peer_of(k):
        return lax.rem(me + k, n_view)

    def push(src, dst, send, recv, k):
        copy = pltpu.make_async_remote_copy(
            src_ref=src, dst_ref=dst, send_sem=send, recv_sem=recv,
            device_id=(tile, peer_of(k)), device_id_type=MESH,
        )
        copy.start()
        return copy

    barrier = pltpu.get_barrier_semaphore()
    for k in range(1, n_view):
        pl.semaphore_signal(barrier, inc=1, device_id=(tile, peer_of(k)), device_id_type=MESH)
    pl.semaphore_wait(barrier, n_view - 1)
    groups = cols // LANES
    order = sorted(range(1, n_view), key=lambda k: -min(k, n_view - k))
    rest = pl.ds(1, n_view - 1)
    for k in order:
        push(sens_ref, rsens.at[k], ssend_sem, srecv_sem, k)
    for g in range(groups):
        piece = pl.ds(per_group * g, per_group)
        for k in order:
            push(back_ref.at[peer_of(k), piece], rback.at[k, piece], send_sem, recv_sem.at[g], k)
    first = pl.multiple_of(me * pc, pc)
    v = vol_ref[pl.ds(first, pc)]
    before = vol_ref[jnp.maximum(first - 1, 0)]
    before = jnp.where(me > 0, before, 0.0)
    after = vol_ref[jnp.minimum(first + pc, planes - 1)]
    after = jnp.where(me < n_view - 1, after, 0.0)
    row = lax.broadcasted_iota(jnp.int32, (pc, rows, cols), 1)
    col = lax.broadcasted_iota(jnp.int32, (pc, rows, cols), 2)
    above = jnp.where(tile > 0, halo_ref[0], 0.0)[:, None, :]
    below = jnp.where(tile < n_tile - 1, halo_ref[1], 0.0)[:, None, :]

    def term(other):
        return jnp.clip(v - other, -HUBER_DELTA, HUBER_DELTA)

    penalty = term(jnp.concatenate([before[None], v[: pc - 1]], axis=0))
    penalty += term(jnp.concatenate([v[1:], after[None]], axis=0))
    penalty += term(jnp.where(row == 0, above, pltpu.roll(v, 1, 1)))
    penalty += term(jnp.where(row == rows - 1, below, pltpu.roll(v, rows - 1, 1)))
    penalty += term(jnp.where(col == 0, 0.0, pltpu.roll(v, 1, 2)))
    penalty += term(jnp.where(col == cols - 1, 0.0, pltpu.roll(v, cols - 1, 2)))
    scale = v / (1.0 + penalty)

    pltpu.make_async_copy(rsens.at[rest], rsens.at[rest], srecv_sem).wait()
    sens = sens_ref[...]
    for k in range(1, n_view):
        sens = sens + rsens[k]

    def finish(g):
        landed = rback.at[rest, pl.ds(per_group * g, per_group)]
        pltpu.make_async_copy(landed, landed, recv_sem.at[g]).wait()
        parts = []
        for j in range(per_group):
            q = per_group * g + j
            total = back_ref[me, q].astype(jnp.float32)
            for k in range(1, n_view):
                total = total + rback[k, q].astype(jnp.float32)
            parts.append(total / sens[q : q + 1])
        for h in range(rows // per_group):
            lanes = slice(LANES * h, LANES * (h + 1))
            for i, out in enumerate(swap_chunks([x[:, lanes] for x in parts], seg_cols)):
                natural[g, pl.ds(per_group * h + i, pc, stride=rows), :] = out
        lanes = slice(LANES * g, LANES * (g + 1))
        out_ref[pl.ds(first, pc), :, lanes] = scale[:, :, lanes] * natural[g].reshape(
            pc, rows, LANES
        )

    def piece_of(owner, g):
        return out_ref.at[pl.ds(pl.multiple_of(owner * pc, pc), pc), :, LANES * g : LANES * (g + 1)]

    far = n_view // 2
    relays = {}

    def relay(side, hop, g):
        owner = lax.rem(me + (n_view - hop if side == 0 else hop), n_view)
        piece = piece_of(owner, g)
        relays[side, hop, g] = push(
            piece, piece, gsend_sem, grecv_sem.at[side, hop, g],
            1 if side == 0 else n_view - 1,
        )

    def reach(side, g):
        return far if (side == 0) == (g < groups // 2) else n_view - 1 - far

    for g in range(groups):
        finish(g)
        for side in (0, 1):
            if reach(side, g) > 0:
                relay(side, 0, g)
    for hop in range(1, far + 1):
        for g in range(groups):
            for side in (0, 1):
                if hop <= reach(side, g):
                    relays[side, hop - 1, g].wait_recv()
                    if hop < reach(side, g):
                        relay(side, hop, g)
    for sent, sem in (
        (rsens.at[rest], ssend_sem),
        (rback.at[rest], send_sem),
        (out_ref.at[pl.ds(0, planes - pc)], gsend_sem),
    ):
        pltpu.make_async_copy(sent, sent, sem).wait()


def per_device(volume, weights, measured, crossings, counts):
    n_tile = lax.axis_size("tile")
    n_view = lax.axis_size("view")
    planes, rows, cols = volume.shape
    views, slots, bins, seg_pixels = weights.shape[1:]
    seg_cols = seg_pixels // rows
    seg_total = cols // seg_cols
    blocks_view = n_tile // views
    pc = planes // n_view
    half = bins // 2
    total = views * blocks_view
    dims = (planes, rows, cols, seg_cols, views, slots, blocks_view, bins, pc)
    f32, bf16 = jnp.float32, jnp.bfloat16
    vmem = pl.BlockSpec(memory_space=pltpu.VMEM)
    smem = pl.BlockSpec(memory_space=pltpu.SMEM)
    dma = pltpu.SemaphoreType.DMA
    local = pltpu.CompilerParams(vmem_limit_bytes=VMEM_LIMIT)

    def remote(number):
        return pltpu.CompilerParams(
            vmem_limit_bytes=VMEM_LIMIT, collective_id=number, has_side_effects=True
        )

    cross = crossings[0].transpose(0, 2, 1).reshape(views * 2 * slots)
    count = counts[0]
    slot_weights = weights.reshape(views * slots, bins, seg_pixels)
    dense, edges = pl.pallas_call(
        functools.partial(forward_kernel, dims),
        out_shape=(
            jax.ShapeDtypeStruct((total, half, LANES), bf16),
            jax.ShapeDtypeStruct((2, pc, cols), f32),
        ),
        in_specs=[smem, smem, vmem, vmem],
        out_specs=(vmem, vmem),
        scratch_shapes=[
            pltpu.VMEM((cols // LANES, planes * rows, LANES), f32),
            pltpu.VMEM((seg_total, 2 * planes, seg_pixels), bf16),
            pltpu.VMEM((total + 1, half, LANES), f32),
        ],
        compiler_params=local,
        name="forward",
    )(cross, count, volume.reshape(planes * rows, cols), slot_weights)
    ratios, halo = pl.pallas_call(
        functools.partial(exchange_kernel, n_tile),
        out_shape=(
            jax.ShapeDtypeStruct((total, half, LANES), bf16),
            jax.ShapeDtypeStruct((2, pc, cols), f32),
        ),
        in_specs=[vmem, vmem, vmem],
        out_specs=(vmem, vmem),
        scratch_shapes=[
            pltpu.VMEM((n_tile, half, LANES), bf16),
            dma, dma, dma, dma, dma((2,)), dma((2,)),
        ],
        compiler_params=remote(1),
        name="exchange",
    )(dense, measured[0, 0, 0].T, edges)
    back, sens = pl.pallas_call(
        functools.partial(backward_kernel, dims),
        out_shape=(
            jax.ShapeDtypeStruct((n_view, seg_total, pc, seg_pixels), bf16),
            jax.ShapeDtypeStruct((seg_total, seg_pixels), f32),
        ),
        in_specs=[smem, smem, vmem, vmem],
        out_specs=(vmem, vmem),
        scratch_shapes=[
            pltpu.VMEM((total + 1, planes + 8, bins), bf16),
            pltpu.VMEM((seg_total, planes + 8, seg_pixels), f32),
        ],
        compiler_params=local,
        name="backward",
    )(cross, count, ratios, slot_weights)
    return pl.pallas_call(
        functools.partial(update_kernel, (n_tile, n_view, seg_cols)),
        out_shape=jax.ShapeDtypeStruct((planes, rows, cols), f32),
        in_specs=[vmem, vmem, vmem, vmem],
        out_specs=vmem,
        scratch_shapes=[
            pltpu.VMEM((n_view, seg_total, pc, seg_pixels), bf16),
            pltpu.VMEM((n_view, seg_total, seg_pixels), f32),
            pltpu.VMEM((cols // LANES, pc * rows, LANES), f32),
        ]
        + [dma, dma, dma, dma, dma((cols // LANES,)), dma((2, n_view // 2, cols // LANES))],
        compiler_params=remote(2),
        name="update",
    )(back, sens, volume, halo)


def solution(mesh):
    in_specs = (
        P(None, "tile", None),
        P("tile", "view", None, None, None),
        P("tile", "view", None, None, None),
        P("tile", "view", None, None),
        P("tile", "view"),
    )
    out_specs = P(None, "tile", None)
    return jax.shard_map(
        per_device, mesh=mesh, in_specs=in_specs, out_specs=out_specs, check_vma=False
    )
```

```python
import functools

import jax
import jax.numpy as jnp
from jax import lax
from jax.experimental import pallas as pl
from jax.experimental.pallas import tpu as pltpu
from jax.sharding import PartitionSpec as P

BACKGROUND = 1.0
HUBER_DELTA = 0.1
LANES = 128
UNROLL = 8
MESH = pl.DeviceIdType.MESH
VMEM_LIMIT = 24 * 1024 * 1024


def lane_block(shape, width):
    return lax.broadcasted_iota(jnp.int32, shape, len(shape) - 1) // width


def swap_chunks(parts, width):
    chunks = len(parts)
    which = lane_block(parts[0].shape, width)
    outs = []
    for i in range(chunks):
        out = parts[i]
        for j in range(chunks):
            if j != i:
                moved = pltpu.roll(parts[j], ((j - i) * width) % LANES, 1)
                out = jnp.where(which == j, moved, out)
        outs.append(out)
    return outs


def forward_kernel(
    dims, cross_ref, counts_ref, vol_ref, w_ref, dense_ref, edges_ref, lists_ref, vol, segs, acc, used
):
    planes, rows, cols, seg_cols, views, slots, blocks_view, bins, pc = dims
    per_group = LANES // seg_cols
    half = bins // 2
    total_blocks = views * blocks_view
    seg_total = cols // seg_cols
    room = 2 * views
    size = seg_total * room + LANES
    for q in range(seg_total):
        used[q] = 0

    def clear(i, carry):
        for u in range(UNROLL):
            lists_ref[i * UNROLL + u] = 0
            lists_ref[size + i * UNROLL + u] = total_blocks
        return carry

    lax.fori_loop(0, seg_total * room // UNROLL, clear, 0)
    first_plane = lax.axis_index("view") * pc
    base = pl.multiple_of(first_plane * rows, rows)
    for g in range(cols // LANES):
        group = slice(LANES * g, LANES * (g + 1))
        vol[g] = vol_ref[:, group]
        edges_ref[0, :, group] = vol[g, pl.ds(base + rows - 1, pc, stride=rows), :]
        edges_ref[1, :, group] = vol[g, pl.ds(base, pc, stride=rows), :]
        for h in range(rows // per_group):
            parts = [
                vol[g, pl.ds(per_group * h + i, planes, stride=rows), :]
                for i in range(per_group)
            ]
            for j, out in enumerate(swap_chunks(parts, seg_cols)):
                out = out.astype(jnp.bfloat16)
                lanes = slice(LANES * h, LANES * (h + 1))
                segs[per_group * g + j, 0:planes, lanes] = out
                segs[per_group * g + j, planes : 2 * planes, lanes] = out
    acc[...] = jnp.zeros_like(acc)
    low = lax.broadcasted_iota(jnp.int32, (half, LANES), 1) < planes

    for w in range(views):
        count = counts_ref[w]

        def body(step, carry, w=w, count=count):
            packed = []
            for u in range(UNROLL):
                k = step * UNROLL + u
                seg = cross_ref[w * 2 * slots + slots + k]
                part = lax.dot_general(
                    w_ref[w * slots + k],
                    segs[seg],
                    (((1,), (1,)), ((), ())),
                    preferred_element_type=jnp.float32,
                )
                packed.append(jnp.where(low, part[:half], part[half:]))
            for u in range(UNROLL):
                k = step * UNROLL + u
                block = cross_ref[w * 2 * slots + k] + w * blocks_view
                at = jnp.where(k < count, block, total_blocks)
                acc[at] += packed[u]
                seg = cross_ref[w * 2 * slots + slots + k]
                place = used[seg]
                used[seg] = place + jnp.where(k < count, 1, 0)
                place = jnp.where(k < count, seg * room + place, seg_total * room)
                lists_ref[place] = w * slots + k
                lists_ref[size + place] = block
            return carry

        lax.fori_loop(0, (count + UNROLL - 1) // UNROLL, body, 0)
    dense_ref[...] = acc[0:total_blocks].astype(jnp.bfloat16)


def exchange_kernel(
    n_tile, dense_ref, meas_ref, edges_ref, ratios_ref, halo_ref, recv,
    send_sem, recv_sem, gsend_sem, grecv_sem, hsend_sem, hrecv_sem,
):
    me = lax.axis_index("tile")
    view = lax.axis_index("view")
    planes = meas_ref.shape[1]
    half = meas_ref.shape[0] // 2

    def peer_of(k):
        return lax.rem(me + k, n_tile)

    barrier = pltpu.get_barrier_semaphore()

    def greet(k, carry):
        pl.semaphore_signal(barrier, inc=1, device_id=(peer_of(k), view), device_id_type=MESH)
        return carry

    lax.fori_loop(1, n_tile, greet, 0)
    pl.semaphore_wait(barrier, n_tile - 1)

    def send(k, carry):
        peer = peer_of(k)
        pltpu.make_async_remote_copy(
            src_ref=dense_ref.at[peer],
            dst_ref=recv.at[k],
            send_sem=send_sem,
            recv_sem=recv_sem,
            device_id=(peer, view),
            device_id_type=MESH,
        ).start()
        return carry

    lax.fori_loop(1, n_tile, send, 0)
    halos = []
    for side, step in ((0, 1), (1, n_tile - 1)):
        halos.append(
            pltpu.make_async_remote_copy(
                src_ref=edges_ref.at[side],
                dst_ref=halo_ref.at[side],
                send_sem=hsend_sem.at[side],
                recv_sem=hrecv_sem.at[side],
                device_id=(peer_of(step), view),
                device_id_type=MESH,
            )
        )
        halos[-1].start()
    low = lax.broadcasted_iota(jnp.int32, (half, LANES), 1) < planes
    counted = jnp.concatenate([meas_ref[...], meas_ref[...]], axis=1)
    counted = jnp.where(low, counted[:half], counted[half:])
    own = dense_ref[me].astype(jnp.float32)
    rest = pl.ds(1, n_tile - 1)
    pltpu.make_async_copy(recv.at[rest], recv.at[rest], recv_sem).wait()
    total = own
    for k in range(1, n_tile):
        total = total + recv[k].astype(jnp.float32)
    ratio = (counted / (total + BACKGROUND)).astype(jnp.bfloat16)
    ratios_ref[me] = ratio

    def spread(k, carry):
        pltpu.make_async_remote_copy(
            src_ref=ratios_ref.at[me],
            dst_ref=ratios_ref.at[me],
            send_sem=gsend_sem,
            recv_sem=grecv_sem,
            device_id=(peer_of(k), view),
            device_id_type=MESH,
        ).start()
        return carry

    lax.fori_loop(1, n_tile, spread, 0)
    pltpu.make_async_copy(recv.at[rest], recv.at[rest], grecv_sem).wait()
    pltpu.make_async_copy(recv.at[rest], recv.at[rest], send_sem).wait()
    pltpu.make_async_copy(recv.at[rest], recv.at[rest], gsend_sem).wait()
    for copy in halos:
        copy.wait()


def update_kernel(
    sizes, lists_ref, ratios_ref, w_ref, vol_ref, halo_ref, out_ref,
    lhs, back_ref, sens_ref, rback, rsens, natural,
    send_sem, ssend_sem, srecv_sem, gsend_sem, recv_sem, grecv_sem,
):
    n_tile, n_view, seg_cols, room = sizes
    tile = lax.axis_index("tile")
    me = lax.axis_index("view")
    planes, rows, cols = vol_ref.shape
    pc = planes // n_view
    per_group = LANES // seg_cols

    def peer_of(k):
        return lax.rem(me + k, n_view)

    def push(src, dst, send, recv, k):
        copy = pltpu.make_async_remote_copy(
            src_ref=src, dst_ref=dst, send_sem=send, recv_sem=recv,
            device_id=(tile, peer_of(k)), device_id_type=MESH,
        )
        copy.start()
        return copy

    barrier = pltpu.get_barrier_semaphore()
    for k in range(1, n_view):
        pl.semaphore_signal(barrier, inc=1, device_id=(tile, peer_of(k)), device_id_type=MESH)
    groups = cols // LANES
    total_blocks = ratios_ref.shape[0]
    bins = w_ref.shape[1]
    size = lists_ref.shape[0] // 2

    def fill(step, carry):
        for u in range(UNROLL):
            b = step * UNROLL + u
            x = ratios_ref[b].astype(jnp.float32)
            x = jnp.concatenate([x, pltpu.roll(x, planes, 1)], axis=0)
            lhs[b, 0:planes] = jnp.transpose(x)[0:planes].astype(jnp.bfloat16)
            lhs[b, planes:] = jnp.ones((lhs.shape[1] - planes, bins), jnp.bfloat16)
        return carry

    lax.fori_loop(0, total_blocks // UNROLL, fill, 0)
    lhs[total_blocks] = jnp.zeros(lhs.shape[1:], jnp.bfloat16)

    def project(q, carry):
        total = jnp.zeros((lhs.shape[1], w_ref.shape[2]), jnp.float32)
        for j in range(room):
            total = total + jnp.dot(
                lhs[lists_ref[size + q * room + j]],
                w_ref[lists_ref[q * room + j]],
                preferred_element_type=jnp.float32,
            )
        for c in range(n_view):
            back_ref[c, q] = total[c * pc : (c + 1) * pc].astype(jnp.bfloat16)
        sens_ref[pl.ds(q, 1)] = total[planes : planes + 1]
        return carry

    order = sorted(range(1, n_view), key=lambda k: -min(k, n_view - k))
    rest = pl.ds(1, n_view - 1)
    for g in range(groups):
        lax.fori_loop(per_group * g, per_group * (g + 1), project, 0)
        if g == 0:
            pl.semaphore_wait(barrier, n_view - 1)
        piece = pl.ds(per_group * g, per_group)
        for k in order:
            push(back_ref.at[peer_of(k), piece], rback.at[k, piece], send_sem, recv_sem.at[g], k)
        if g % 2 == 1:
            part = pl.ds(per_group * (g - 1), 2 * per_group)
            for k in order:
                push(sens_ref.at[part], rsens.at[k, part], ssend_sem, srecv_sem.at[g // 2], k)
    first = pl.multiple_of(me * pc, pc)
    v = vol_ref[pl.ds(first, pc)]
    before = vol_ref[jnp.maximum(first - 1, 0)]
    before = jnp.where(me > 0, before, 0.0)
    after = vol_ref[jnp.minimum(first + pc, planes - 1)]
    after = jnp.where(me < n_view - 1, after, 0.0)
    row = lax.broadcasted_iota(jnp.int32, (pc, rows, cols), 1)
    col = lax.broadcasted_iota(jnp.int32, (pc, rows, cols), 2)
    above = jnp.where(tile > 0, halo_ref[0], 0.0)[:, None, :]
    below = jnp.where(tile < n_tile - 1, halo_ref[1], 0.0)[:, None, :]

    def term(other):
        return jnp.clip(v - other, -HUBER_DELTA, HUBER_DELTA)

    penalty = term(jnp.concatenate([before[None], v[: pc - 1]], axis=0))
    penalty += term(jnp.concatenate([v[1:], after[None]], axis=0))
    penalty += term(jnp.where(row == 0, above, pltpu.roll(v, 1, 1)))
    penalty += term(jnp.where(row == rows - 1, below, pltpu.roll(v, rows - 1, 1)))
    penalty += term(jnp.where(col == 0, 0.0, pltpu.roll(v, 1, 2)))
    penalty += term(jnp.where(col == cols - 1, 0.0, pltpu.roll(v, cols - 1, 2)))
    scale = v / (1.0 + penalty)

    sens_of = {}

    def sens_total(g):
        if g not in sens_of:
            part = pl.ds(per_group * g, 2 * per_group)
            landed = rsens.at[rest, part]
            pltpu.make_async_copy(landed, landed, srecv_sem.at[g // 2]).wait()
            sens = sens_ref[part]
            for k in range(1, n_view):
                sens = sens + rsens[k, part]
            sens_of[g] = sens
        return sens_of[g]

    def finish(g):
        landed = rback.at[rest, pl.ds(per_group * g, per_group)]
        pltpu.make_async_copy(landed, landed, recv_sem.at[g]).wait()
        sens = sens_total(g - g % 2)
        parts = []
        for j in range(per_group):
            q = per_group * g + j
            total = back_ref[me, q].astype(jnp.float32)
            for k in range(1, n_view):
                total = total + rback[k, q].astype(jnp.float32)
            at = per_group * (g % 2) + j
            parts.append(total / sens[at : at + 1])
        for h in range(rows // per_group):
            lanes = slice(LANES * h, LANES * (h + 1))
            for i, out in enumerate(swap_chunks([x[:, lanes] for x in parts], seg_cols)):
                natural[g, pl.ds(per_group * h + i, pc, stride=rows), :] = out
        lanes = slice(LANES * g, LANES * (g + 1))
        out_ref[pl.ds(first, pc), :, lanes] = scale[:, :, lanes] * natural[g].reshape(
            pc, rows, LANES
        )

    def piece_of(owner, g):
        return out_ref.at[pl.ds(pl.multiple_of(owner * pc, pc), pc), :, LANES * g : LANES * (g + 1)]

    far = n_view // 2
    relays = {}

    def relay(side, hop, g):
        owner = lax.rem(me + (n_view - hop if side == 0 else hop), n_view)
        piece = piece_of(owner, g)
        relays[side, hop, g] = push(
            piece, piece, gsend_sem, grecv_sem.at[side, hop, g],
            1 if side == 0 else n_view - 1,
        )

    def reach(side, g):
        return far if (side == 0) == (g < groups // 2) else n_view - 1 - far

    for g in range(groups):
        finish(g)
        for side in (0, 1):
            if reach(side, g) > 0:
                relay(side, 0, g)
    for hop in range(1, far + 1):
        for g in range(groups):
            for side in (0, 1):
                if hop <= reach(side, g):
                    relays[side, hop - 1, g].wait_recv()
                    if hop < reach(side, g):
                        relay(side, hop, g)
    for sent, sem in (
        (rsens.at[rest], ssend_sem),
        (rback.at[rest], send_sem),
        (out_ref.at[pl.ds(0, planes - pc)], gsend_sem),
    ):
        pltpu.make_async_copy(sent, sent, sem).wait()


def per_device(volume, weights, measured, crossings, counts):
    n_tile = lax.axis_size("tile")
    n_view = lax.axis_size("view")
    planes, rows, cols = volume.shape
    views, slots, bins, seg_pixels = weights.shape[1:]
    seg_cols = seg_pixels // rows
    seg_total = cols // seg_cols
    blocks_view = n_tile // views
    pc = planes // n_view
    half = bins // 2
    total = views * blocks_view
    dims = (planes, rows, cols, seg_cols, views, slots, blocks_view, bins, pc)
    f32, bf16 = jnp.float32, jnp.bfloat16
    vmem = pl.BlockSpec(memory_space=pltpu.VMEM)
    smem = pl.BlockSpec(memory_space=pltpu.SMEM)
    dma = pltpu.SemaphoreType.DMA
    local = pltpu.CompilerParams(vmem_limit_bytes=VMEM_LIMIT)

    def remote(number):
        return pltpu.CompilerParams(
            vmem_limit_bytes=VMEM_LIMIT, collective_id=number, has_side_effects=True
        )

    cross = crossings[0].transpose(0, 2, 1).reshape(views * 2 * slots)
    count = counts[0]
    slot_weights = weights.reshape(views * slots, bins, seg_pixels)
    dense, edges, lists = pl.pallas_call(
        functools.partial(forward_kernel, dims),
        out_shape=(
            jax.ShapeDtypeStruct((total, half, LANES), bf16),
            jax.ShapeDtypeStruct((2, pc, cols), f32),
            jax.ShapeDtypeStruct((2 * (seg_total * 2 * views + LANES),), jnp.int32),
        ),
        in_specs=[smem, smem, vmem, vmem],
        out_specs=(vmem, vmem, smem),
        scratch_shapes=[
            pltpu.VMEM((cols // LANES, planes * rows, LANES), f32),
            pltpu.VMEM((seg_total, 2 * planes, seg_pixels), bf16),
            pltpu.VMEM((total + 1, half, LANES), f32),
            pltpu.SMEM((seg_total,), jnp.int32),
        ],
        compiler_params=local,
        name="forward",
    )(cross, count, volume.reshape(planes * rows, cols), slot_weights)
    ratios, halo = pl.pallas_call(
        functools.partial(exchange_kernel, n_tile),
        out_shape=(
            jax.ShapeDtypeStruct((total, half, LANES), bf16),
            jax.ShapeDtypeStruct((2, pc, cols), f32),
        ),
        in_specs=[vmem, vmem, vmem],
        out_specs=(vmem, vmem),
        scratch_shapes=[
            pltpu.VMEM((n_tile, half, LANES), bf16),
            dma, dma, dma, dma, dma((2,)), dma((2,)),
        ],
        compiler_params=remote(1),
        name="exchange",
    )(dense, measured[0, 0, 0].T, edges)
    return pl.pallas_call(
        functools.partial(update_kernel, (n_tile, n_view, seg_cols, 2 * views)),
        out_shape=jax.ShapeDtypeStruct((planes, rows, cols), f32),
        in_specs=[smem, vmem, vmem, vmem, vmem],
        out_specs=vmem,
        scratch_shapes=[
            pltpu.VMEM((total + 1, planes + 8, bins), bf16),
            pltpu.VMEM((n_view, seg_total, pc, seg_pixels), bf16),
            pltpu.VMEM((seg_total, seg_pixels), f32),
            pltpu.VMEM((n_view, seg_total, pc, seg_pixels), bf16),
            pltpu.VMEM((n_view, seg_total, seg_pixels), f32),
            pltpu.VMEM((cols // LANES, pc * rows, LANES), f32),
        ]
        + [dma, dma, dma((cols // LANES // 2,)), dma, dma((cols // LANES,)), dma((2, n_view // 2, cols // LANES))],
        compiler_params=remote(2),
        name="update",
    )(lists, ratios, slot_weights, volume, halo)


def solution(mesh):
    in_specs = (
        P(None, "tile", None),
        P("tile", "view", None, None, None),
        P("tile", "view", None, None, None),
        P("tile", "view", None, None),
        P("tile", "view"),
    )
    out_specs = P(None, "tile", None)
    return jax.shard_map(
        per_device, mesh=mesh, in_specs=in_specs, out_specs=out_specs, check_vma=False
    )
```

```python
import functools

import jax
import jax.numpy as jnp
from jax import lax
from jax.experimental import pallas as pl
from jax.experimental.pallas import tpu as pltpu
from jax.sharding import PartitionSpec as P

BACKGROUND = 1.0
HUBER_DELTA = 0.1
LANES = 128
UNROLL = 8
MESH = pl.DeviceIdType.MESH
VMEM_LIMIT = 24 * 1024 * 1024


def lane_block(shape, width):
    return lax.broadcasted_iota(jnp.int32, shape, len(shape) - 1) // width


def swap_chunks(parts, width):
    chunks = len(parts)
    which = lane_block(parts[0].shape, width)
    outs = []
    for i in range(chunks):
        out = parts[i]
        for j in range(chunks):
            if j != i:
                moved = pltpu.roll(parts[j], ((j - i) * width) % LANES, 1)
                out = jnp.where(which == j, moved, out)
        outs.append(out)
    return outs


def forward_kernel(
    dims, cross_ref, counts_ref, vol_ref, w_ref, dense_ref, edges_ref, lists_ref, vol, segs, acc, used
):
    planes, rows, cols, seg_cols, views, slots, blocks_view, bins, pc = dims
    per_group = LANES // seg_cols
    half = bins // 2
    total_blocks = views * blocks_view
    seg_total = cols // seg_cols
    room = 2 * views
    size = seg_total * room + LANES
    for q in range(seg_total):
        used[q] = 0

    def clear(i, carry):
        for u in range(UNROLL):
            lists_ref[i * UNROLL + u] = 0
            lists_ref[size + i * UNROLL + u] = total_blocks
        return carry

    lax.fori_loop(0, seg_total * room // UNROLL, clear, 0)
    first_plane = lax.axis_index("view") * pc
    base = pl.multiple_of(first_plane * rows, rows)
    for g in range(cols // LANES):
        group = slice(LANES * g, LANES * (g + 1))
        vol[g] = vol_ref[:, group]
        edges_ref[0, :, group] = vol[g, pl.ds(base + rows - 1, pc, stride=rows), :]
        edges_ref[1, :, group] = vol[g, pl.ds(base, pc, stride=rows), :]
        for h in range(rows // per_group):
            parts = [
                vol[g, pl.ds(per_group * h + i, planes, stride=rows), :]
                for i in range(per_group)
            ]
            for j, out in enumerate(swap_chunks(parts, seg_cols)):
                out = out.astype(jnp.bfloat16)
                lanes = slice(LANES * h, LANES * (h + 1))
                segs[per_group * g + j, 0:planes, lanes] = out
                segs[per_group * g + j, planes : 2 * planes, lanes] = out
    acc[...] = jnp.zeros_like(acc)
    low = lax.broadcasted_iota(jnp.int32, (half, LANES), 1) < planes

    for w in range(views):
        count = counts_ref[w]

        def body(step, carry, w=w, count=count):
            packed = []
            for u in range(UNROLL):
                k = step * UNROLL + u
                seg = cross_ref[w * 2 * slots + slots + k]
                part = lax.dot_general(
                    w_ref[w * slots + k],
                    segs[seg],
                    (((1,), (1,)), ((), ())),
                    preferred_element_type=jnp.float32,
                )
                packed.append(jnp.where(low, part[:half], part[half:]))
            for u in range(UNROLL):
                k = step * UNROLL + u
                block = cross_ref[w * 2 * slots + k] + w * blocks_view
                at = jnp.where(k < count, block, total_blocks)
                acc[at] += packed[u]
                seg = cross_ref[w * 2 * slots + slots + k]
                place = used[seg]
                used[seg] = place + jnp.where(k < count, 1, 0)
                place = jnp.where(k < count, seg * room + place, seg_total * room)
                lists_ref[place] = w * slots + k
                lists_ref[size + place] = block
            return carry

        lax.fori_loop(0, (count + UNROLL - 1) // UNROLL, body, 0)
    dense_ref[...] = acc[0:total_blocks].astype(jnp.bfloat16)


def exchange_kernel(
    n_tile, dense_ref, meas_ref, edges_ref, ratios_ref, halo_ref, recv,
    send_sem, recv_sem, gsend_sem, grecv_sem, hsend_sem, hrecv_sem,
):
    me = lax.axis_index("tile")
    view = lax.axis_index("view")
    planes = meas_ref.shape[1]
    half = meas_ref.shape[0] // 2

    def peer_of(k):
        return lax.rem(me + k, n_tile)

    def offset(i):
        return n_tile // 2 + (i + 1) // 2 * (2 * (i % 2) - 1)

    barrier = pltpu.get_barrier_semaphore()

    def greet(k, carry):
        pl.semaphore_signal(barrier, inc=1, device_id=(peer_of(k), view), device_id_type=MESH)
        return carry

    lax.fori_loop(1, n_tile, greet, 0)
    pl.semaphore_wait(barrier, n_tile - 1)

    def send(i, carry):
        k = offset(i)
        peer = peer_of(k)
        pltpu.make_async_remote_copy(
            src_ref=dense_ref.at[peer],
            dst_ref=recv.at[k],
            send_sem=send_sem,
            recv_sem=recv_sem,
            device_id=(peer, view),
            device_id_type=MESH,
        ).start()
        return carry

    lax.fori_loop(0, n_tile - 1, send, 0)
    halos = []
    for side, step in ((0, 1), (1, n_tile - 1)):
        halos.append(
            pltpu.make_async_remote_copy(
                src_ref=edges_ref.at[side],
                dst_ref=halo_ref.at[side],
                send_sem=hsend_sem.at[side],
                recv_sem=hrecv_sem.at[side],
                device_id=(peer_of(step), view),
                device_id_type=MESH,
            )
        )
        halos[-1].start()
    low = lax.broadcasted_iota(jnp.int32, (half, LANES), 1) < planes
    counted = jnp.concatenate([meas_ref[...], meas_ref[...]], axis=1)
    counted = jnp.where(low, counted[:half], counted[half:])
    own = dense_ref[me].astype(jnp.float32)
    rest = pl.ds(1, n_tile - 1)
    pltpu.make_async_copy(recv.at[rest], recv.at[rest], recv_sem).wait()
    total = own
    for k in range(1, n_tile):
        total = total + recv[k].astype(jnp.float32)
    ratio = (counted / (total + BACKGROUND)).astype(jnp.bfloat16)
    ratios_ref[me] = ratio

    def spread(i, carry):
        k = offset(i)
        pltpu.make_async_remote_copy(
            src_ref=ratios_ref.at[me],
            dst_ref=ratios_ref.at[me],
            send_sem=gsend_sem,
            recv_sem=grecv_sem,
            device_id=(peer_of(k), view),
            device_id_type=MESH,
        ).start()
        return carry

    lax.fori_loop(0, n_tile - 1, spread, 0)
    pltpu.make_async_copy(recv.at[rest], recv.at[rest], grecv_sem).wait()
    pltpu.make_async_copy(recv.at[rest], recv.at[rest], send_sem).wait()
    pltpu.make_async_copy(recv.at[rest], recv.at[rest], gsend_sem).wait()
    for copy in halos:
        copy.wait()


def update_kernel(
    sizes, lists_ref, ratios_ref, w_ref, vol_ref, halo_ref, out_ref,
    lhs, back_ref, sens_ref, rback, rsens, natural,
    send_sem, ssend_sem, srecv_sem, gsend_sem, recv_sem, grecv_sem,
):
    n_tile, n_view, seg_cols, room = sizes
    tile = lax.axis_index("tile")
    me = lax.axis_index("view")
    planes, rows, cols = vol_ref.shape
    pc = planes // n_view
    per_group = LANES // seg_cols

    def peer_of(k):
        return lax.rem(me + k, n_view)

    def push(src, dst, send, recv, k):
        copy = pltpu.make_async_remote_copy(
            src_ref=src, dst_ref=dst, send_sem=send, recv_sem=recv,
            device_id=(tile, peer_of(k)), device_id_type=MESH,
        )
        copy.start()
        return copy

    barrier = pltpu.get_barrier_semaphore()
    for k in range(1, n_view):
        pl.semaphore_signal(barrier, inc=1, device_id=(tile, peer_of(k)), device_id_type=MESH)
    groups = cols // LANES
    total_blocks = ratios_ref.shape[0]
    bins = w_ref.shape[1]
    size = lists_ref.shape[0] // 2

    def fill(step, carry):
        for u in range(UNROLL):
            b = step * UNROLL + u
            x = ratios_ref[b].astype(jnp.float32)
            x = jnp.concatenate([x, pltpu.roll(x, planes, 1)], axis=0)
            lhs[b, 0:planes] = jnp.transpose(x)[0:planes].astype(jnp.bfloat16)
            lhs[b, planes:] = jnp.ones((lhs.shape[1] - planes, bins), jnp.bfloat16)
        return carry

    lax.fori_loop(0, total_blocks // UNROLL, fill, 0)
    lhs[total_blocks] = jnp.zeros(lhs.shape[1:], jnp.bfloat16)

    def project(q, carry):
        total = jnp.zeros((lhs.shape[1], w_ref.shape[2]), jnp.float32)
        for j in range(room):
            total = total + jnp.dot(
                lhs[lists_ref[size + q * room + j]],
                w_ref[lists_ref[q * room + j]],
                preferred_element_type=jnp.float32,
            )
        for c in range(n_view):
            back_ref[c, q] = total[c * pc : (c + 1) * pc].astype(jnp.bfloat16)
        sens_ref[pl.ds(q, 1)] = total[planes : planes + 1]
        return carry

    order = sorted(range(1, n_view), key=lambda k: -min(k, n_view - k))
    rest = pl.ds(1, n_view - 1)
    for g in range(groups):
        lax.fori_loop(per_group * g, per_group * (g + 1), project, 0)
        if g == 0:
            pl.semaphore_wait(barrier, n_view - 1)
        piece = pl.ds(per_group * g, per_group)
        for k in order:
            push(back_ref.at[peer_of(k), piece], rback.at[k, piece], send_sem, recv_sem.at[g], k)
        if g % 2 == 1:
            part = pl.ds(per_group * (g - 1), 2 * per_group)
            for k in order:
                push(sens_ref.at[part], rsens.at[k, part], ssend_sem, srecv_sem.at[g // 2], k)
    first = pl.multiple_of(me * pc, pc)
    v = vol_ref[pl.ds(first, pc)]
    before = vol_ref[jnp.maximum(first - 1, 0)]
    before = jnp.where(me > 0, before, 0.0)
    after = vol_ref[jnp.minimum(first + pc, planes - 1)]
    after = jnp.where(me < n_view - 1, after, 0.0)
    row = lax.broadcasted_iota(jnp.int32, (pc, rows, cols), 1)
    col = lax.broadcasted_iota(jnp.int32, (pc, rows, cols), 2)
    above = jnp.where(tile > 0, halo_ref[0], 0.0)[:, None, :]
    below = jnp.where(tile < n_tile - 1, halo_ref[1], 0.0)[:, None, :]

    def term(other):
        return jnp.clip(v - other, -HUBER_DELTA, HUBER_DELTA)

    penalty = term(jnp.concatenate([before[None], v[: pc - 1]], axis=0))
    penalty += term(jnp.concatenate([v[1:], after[None]], axis=0))
    penalty += term(jnp.where(row == 0, above, pltpu.roll(v, 1, 1)))
    penalty += term(jnp.where(row == rows - 1, below, pltpu.roll(v, rows - 1, 1)))
    penalty += term(jnp.where(col == 0, 0.0, pltpu.roll(v, 1, 2)))
    penalty += term(jnp.where(col == cols - 1, 0.0, pltpu.roll(v, cols - 1, 2)))
    scale = v / (1.0 + penalty)

    sens_of = {}

    def sens_total(g):
        if g not in sens_of:
            part = pl.ds(per_group * g, 2 * per_group)
            landed = rsens.at[rest, part]
            pltpu.make_async_copy(landed, landed, srecv_sem.at[g // 2]).wait()
            sens = sens_ref[part]
            for k in range(1, n_view):
                sens = sens + rsens[k, part]
            sens_of[g] = sens
        return sens_of[g]

    def finish(g):
        landed = rback.at[rest, pl.ds(per_group * g, per_group)]
        pltpu.make_async_copy(landed, landed, recv_sem.at[g]).wait()
        sens = sens_total(g - g % 2)
        parts = []
        for j in range(per_group):
            q = per_group * g + j
            total = back_ref[me, q].astype(jnp.float32)
            for k in range(1, n_view):
                total = total + rback[k, q].astype(jnp.float32)
            at = per_group * (g % 2) + j
            parts.append(total / sens[at : at + 1])
        for h in range(rows // per_group):
            lanes = slice(LANES * h, LANES * (h + 1))
            for i, out in enumerate(swap_chunks([x[:, lanes] for x in parts], seg_cols)):
                natural[g, pl.ds(per_group * h + i, pc, stride=rows), :] = out
        lanes = slice(LANES * g, LANES * (g + 1))
        out_ref[pl.ds(first, pc), :, lanes] = scale[:, :, lanes] * natural[g].reshape(
            pc, rows, LANES
        )

    def piece_of(owner, g):
        return out_ref.at[pl.ds(pl.multiple_of(owner * pc, pc), pc), :, LANES * g : LANES * (g + 1)]

    far = n_view // 2
    relays = {}

    def relay(side, hop, g):
        owner = lax.rem(me + (n_view - hop if side == 0 else hop), n_view)
        piece = piece_of(owner, g)
        relays[side, hop, g] = push(
            piece, piece, gsend_sem, grecv_sem.at[side, hop, g],
            1 if side == 0 else n_view - 1,
        )

    def reach(side, g):
        return far if (side == 0) == (g < groups // 2) else n_view - 1 - far

    for g in range(groups):
        finish(g)
        for side in (0, 1):
            if reach(side, g) > 0:
                relay(side, 0, g)
    for hop in range(1, far + 1):
        for g in range(groups):
            for side in (0, 1):
                if hop <= reach(side, g):
                    relays[side, hop - 1, g].wait_recv()
                    if hop < reach(side, g):
                        relay(side, hop, g)
    for sent, sem in (
        (rsens.at[rest], ssend_sem),
        (rback.at[rest], send_sem),
        (out_ref.at[pl.ds(0, planes - pc)], gsend_sem),
    ):
        pltpu.make_async_copy(sent, sent, sem).wait()


def per_device(volume, weights, measured, crossings, counts):
    n_tile = lax.axis_size("tile")
    n_view = lax.axis_size("view")
    planes, rows, cols = volume.shape
    views, slots, bins, seg_pixels = weights.shape[1:]
    seg_cols = seg_pixels // rows
    seg_total = cols // seg_cols
    blocks_view = n_tile // views
    pc = planes // n_view
    half = bins // 2
    total = views * blocks_view
    dims = (planes, rows, cols, seg_cols, views, slots, blocks_view, bins, pc)
    f32, bf16 = jnp.float32, jnp.bfloat16
    vmem = pl.BlockSpec(memory_space=pltpu.VMEM)
    smem = pl.BlockSpec(memory_space=pltpu.SMEM)
    dma = pltpu.SemaphoreType.DMA
    local = pltpu.CompilerParams(vmem_limit_bytes=VMEM_LIMIT)

    def remote(number):
        return pltpu.CompilerParams(
            vmem_limit_bytes=VMEM_LIMIT, collective_id=number, has_side_effects=True
        )

    cross = crossings[0].transpose(0, 2, 1).reshape(views * 2 * slots)
    count = counts[0]
    slot_weights = weights.reshape(views * slots, bins, seg_pixels)
    dense, edges, lists = pl.pallas_call(
        functools.partial(forward_kernel, dims),
        out_shape=(
            jax.ShapeDtypeStruct((total, half, LANES), bf16),
            jax.ShapeDtypeStruct((2, pc, cols), f32),
            jax.ShapeDtypeStruct((2 * (seg_total * 2 * views + LANES),), jnp.int32),
        ),
        in_specs=[smem, smem, vmem, vmem],
        out_specs=(vmem, vmem, smem),
        scratch_shapes=[
            pltpu.VMEM((cols // LANES, planes * rows, LANES), f32),
            pltpu.VMEM((seg_total, 2 * planes, seg_pixels), bf16),
            pltpu.VMEM((total + 1, half, LANES), f32),
            pltpu.SMEM((seg_total,), jnp.int32),
        ],
        compiler_params=local,
        name="forward",
    )(cross, count, volume.reshape(planes * rows, cols), slot_weights)
    ratios, halo = pl.pallas_call(
        functools.partial(exchange_kernel, n_tile),
        out_shape=(
            jax.ShapeDtypeStruct((total, half, LANES), bf16),
            jax.ShapeDtypeStruct((2, pc, cols), f32),
        ),
        in_specs=[vmem, vmem, vmem],
        out_specs=(vmem, vmem),
        scratch_shapes=[
            pltpu.VMEM((n_tile, half, LANES), bf16),
            dma, dma, dma, dma, dma((2,)), dma((2,)),
        ],
        compiler_params=remote(1),
        name="exchange",
    )(dense, measured[0, 0, 0].T, edges)
    return pl.pallas_call(
        functools.partial(update_kernel, (n_tile, n_view, seg_cols, 2 * views)),
        out_shape=jax.ShapeDtypeStruct((planes, rows, cols), f32),
        in_specs=[smem, vmem, vmem, vmem, vmem],
        out_specs=vmem,
        scratch_shapes=[
            pltpu.VMEM((total + 1, planes + 8, bins), bf16),
            pltpu.VMEM((n_view, seg_total, pc, seg_pixels), bf16),
            pltpu.VMEM((seg_total, seg_pixels), f32),
            pltpu.VMEM((n_view, seg_total, pc, seg_pixels), bf16),
            pltpu.VMEM((n_view, seg_total, seg_pixels), f32),
            pltpu.VMEM((cols // LANES, pc * rows, LANES), f32),
        ]
        + [dma, dma, dma((cols // LANES // 2,)), dma, dma((cols // LANES,)), dma((2, n_view // 2, cols // LANES))],
        compiler_params=remote(2),
        name="update",
    )(lists, ratios, slot_weights, volume, halo)


def solution(mesh):
    in_specs = (
        P(None, "tile", None),
        P("tile", "view", None, None, None),
        P("tile", "view", None, None, None),
        P("tile", "view", None, None),
        P("tile", "view"),
    )
    out_specs = P(None, "tile", None)
    return jax.shard_map(
        per_device, mesh=mesh, in_specs=in_specs, out_specs=out_specs, check_vma=False
    )
```

```python
import functools

import jax
import jax.numpy as jnp
from jax import lax
from jax.experimental import pallas as pl
from jax.experimental.pallas import tpu as pltpu
from jax.sharding import PartitionSpec as P

BACKGROUND = 1.0
HUBER_DELTA = 0.1
LANES = 128
UNROLL = 8
MESH = pl.DeviceIdType.MESH
VMEM_LIMIT = 24 * 1024 * 1024


def lane_block(shape, width):
    return lax.broadcasted_iota(jnp.int32, shape, len(shape) - 1) // width


def swap_chunks(parts, width):
    chunks = len(parts)
    which = lane_block(parts[0].shape, width)
    outs = []
    for i in range(chunks):
        out = parts[i]
        for j in range(chunks):
            if j != i:
                moved = pltpu.roll(parts[j], ((j - i) * width) % LANES, 1)
                out = jnp.where(which == j, moved, out)
        outs.append(out)
    return outs


def forward_kernel(
    dims, cross_ref, counts_ref, vol_ref, w_ref, dense_ref, edges_ref, lists_ref,
    sens_ref, vol, segs, acc, used, sums,
):
    planes, rows, cols, seg_cols, views, slots, blocks_view, bins, pc = dims
    per_group = LANES // seg_cols
    half = bins // 2
    total_blocks = views * blocks_view
    seg_total = cols // seg_cols
    room = 2 * views
    size = seg_total * room + LANES
    for q in range(seg_total):
        used[q] = 0

    def clear(i, carry):
        for u in range(UNROLL):
            lists_ref[i * UNROLL + u] = 0
            lists_ref[size + i * UNROLL + u] = total_blocks
        return carry

    lax.fori_loop(0, seg_total * room // UNROLL, clear, 0)
    first_plane = lax.axis_index("view") * pc
    base = pl.multiple_of(first_plane * rows, rows)
    for g in range(cols // LANES):
        group = slice(LANES * g, LANES * (g + 1))
        vol[g] = vol_ref[:, group]
        edges_ref[0, :, group] = vol[g, pl.ds(base + rows - 1, pc, stride=rows), :]
        edges_ref[1, :, group] = vol[g, pl.ds(base, pc, stride=rows), :]
        for h in range(rows // per_group):
            parts = [
                vol[g, pl.ds(per_group * h + i, planes, stride=rows), :]
                for i in range(per_group)
            ]
            for j, out in enumerate(swap_chunks(parts, seg_cols)):
                out = out.astype(jnp.bfloat16)
                lanes = slice(LANES * h, LANES * (h + 1))
                segs[per_group * g + j, 0:planes, lanes] = out
                segs[per_group * g + j, planes : 2 * planes, lanes] = out
    acc[...] = jnp.zeros_like(acc)
    sums[...] = jnp.zeros_like(sums)
    low = lax.broadcasted_iota(jnp.int32, (half, LANES), 1) < planes

    for w in range(views):
        count = counts_ref[w]

        def body(step, carry, w=w, count=count):
            packed = []
            for u in range(UNROLL):
                k = step * UNROLL + u
                seg = cross_ref[w * 2 * slots + slots + k]
                part = lax.dot_general(
                    w_ref[w * slots + k],
                    segs[seg],
                    (((1,), (1,)), ((), ())),
                    preferred_element_type=jnp.float32,
                )
                packed.append(jnp.where(low, part[:half], part[half:]))
            for u in range(UNROLL):
                k = step * UNROLL + u
                block = cross_ref[w * 2 * slots + k] + w * blocks_view
                at = jnp.where(k < count, block, total_blocks)
                acc[at] += packed[u]
                seg = cross_ref[w * 2 * slots + slots + k]
                place = used[seg]
                used[seg] = place + jnp.where(k < count, 1, 0)
                place = jnp.where(k < count, seg * room + place, seg_total * room)
                lists_ref[place] = w * slots + k
                lists_ref[size + place] = block
                tall = w_ref[w * slots + k].astype(jnp.float32).reshape(bins // 8, 8, -1)
                sums[jnp.where(k < count, seg, seg_total)] += jnp.sum(tall, axis=0)
            return carry

        lax.fori_loop(0, (count + UNROLL - 1) // UNROLL, body, 0)
    dense_ref[...] = acc[0:total_blocks].astype(jnp.bfloat16)
    sens_ref[...] = jnp.sum(sums[0:seg_total], axis=1)


def exchange_kernel(
    n_tile, n_view, dense_ref, meas_ref, edges_ref, sens_ref, ratios_ref, halo_ref, rsens_ref, recv,
    send_sem, recv_sem, gsend_sem, grecv_sem, ssend_sem, srecv_sem, hsend_sem, hrecv_sem,
):
    me = lax.axis_index("tile")
    view = lax.axis_index("view")
    planes = meas_ref.shape[1]
    half = meas_ref.shape[0] // 2

    def peer_of(k):
        return lax.rem(me + k, n_tile)

    barrier = pltpu.get_barrier_semaphore()

    def greet(k, carry):
        pl.semaphore_signal(barrier, inc=1, device_id=(peer_of(k), view), device_id_type=MESH)
        return carry

    lax.fori_loop(1, n_tile, greet, 0)
    for k in range(1, n_view):
        above = lax.rem(view + k, n_view)
        pl.semaphore_signal(barrier, inc=1, device_id=(me, above), device_id_type=MESH)
    rsens_ref[0] = sens_ref[...]
    pl.semaphore_wait(barrier, n_tile + n_view - 2)

    def send(k, carry):
        peer = peer_of(k)
        pltpu.make_async_remote_copy(
            src_ref=dense_ref.at[peer],
            dst_ref=recv.at[k],
            send_sem=send_sem,
            recv_sem=recv_sem,
            device_id=(peer, view),
            device_id_type=MESH,
        ).start()
        return carry

    lax.fori_loop(1, n_tile, send, 0)
    for k in range(1, n_view):
        pltpu.make_async_remote_copy(
            src_ref=sens_ref,
            dst_ref=rsens_ref.at[k],
            send_sem=ssend_sem,
            recv_sem=srecv_sem,
            device_id=(me, lax.rem(view + k, n_view)),
            device_id_type=MESH,
        ).start()
    halos = []
    for side, step in ((0, 1), (1, n_tile - 1)):
        halos.append(
            pltpu.make_async_remote_copy(
                src_ref=edges_ref.at[side],
                dst_ref=halo_ref.at[side],
                send_sem=hsend_sem.at[side],
                recv_sem=hrecv_sem.at[side],
                device_id=(peer_of(step), view),
                device_id_type=MESH,
            )
        )
        halos[-1].start()
    low = lax.broadcasted_iota(jnp.int32, (half, LANES), 1) < planes
    counted = jnp.concatenate([meas_ref[...], meas_ref[...]], axis=1)
    counted = jnp.where(low, counted[:half], counted[half:])
    own = dense_ref[me].astype(jnp.float32)
    rest = pl.ds(1, n_tile - 1)
    pltpu.make_async_copy(recv.at[rest], recv.at[rest], recv_sem).wait()
    total = own
    for k in range(1, n_tile):
        total = total + recv[k].astype(jnp.float32)
    ratio = (counted / (total + BACKGROUND)).astype(jnp.bfloat16)
    ratios_ref[me] = ratio

    def spread(k, carry):
        pltpu.make_async_remote_copy(
            src_ref=ratios_ref.at[me],
            dst_ref=ratios_ref.at[me],
            send_sem=gsend_sem,
            recv_sem=grecv_sem,
            device_id=(peer_of(k), view),
            device_id_type=MESH,
        ).start()
        return carry

    lax.fori_loop(1, n_tile, spread, 0)
    pltpu.make_async_copy(recv.at[rest], recv.at[rest], grecv_sem).wait()
    pltpu.make_async_copy(recv.at[rest], recv.at[rest], send_sem).wait()
    pltpu.make_async_copy(recv.at[rest], recv.at[rest], gsend_sem).wait()
    for copy in halos:
        copy.wait()
    others = rsens_ref.at[pl.ds(1, n_view - 1)]
    pltpu.make_async_copy(others, others, srecv_sem).wait()
    pltpu.make_async_copy(others, others, ssend_sem).wait()


def update_kernel(
    sizes, lists_ref, ratios_ref, w_ref, vol_ref, halo_ref, rsens, out_ref,
    lhs, back_ref, rback, natural,
    send_sem, gsend_sem, recv_sem, grecv_sem,
):
    n_tile, n_view, seg_cols, room = sizes
    tile = lax.axis_index("tile")
    me = lax.axis_index("view")
    planes, rows, cols = vol_ref.shape
    pc = planes // n_view
    per_group = LANES // seg_cols

    def peer_of(k):
        return lax.rem(me + k, n_view)

    def push(src, dst, send, recv, k):
        copy = pltpu.make_async_remote_copy(
            src_ref=src, dst_ref=dst, send_sem=send, recv_sem=recv,
            device_id=(tile, peer_of(k)), device_id_type=MESH,
        )
        copy.start()
        return copy

    barrier = pltpu.get_barrier_semaphore()
    for k in range(1, n_view):
        pl.semaphore_signal(barrier, inc=1, device_id=(tile, peer_of(k)), device_id_type=MESH)
    groups = cols // LANES
    total_blocks = ratios_ref.shape[0]
    size = lists_ref.shape[0] // 2

    def fill(step, carry):
        for u in range(UNROLL):
            b = step * UNROLL + u
            x = ratios_ref[b].astype(jnp.float32)
            x = jnp.concatenate([x, pltpu.roll(x, planes, 1)], axis=0)
            lhs[b] = jnp.transpose(x)[0:planes].astype(jnp.bfloat16)
        return carry

    lax.fori_loop(0, total_blocks // UNROLL, fill, 0)
    lhs[total_blocks] = jnp.zeros(lhs.shape[1:], jnp.bfloat16)

    def project(q, carry):
        total = jnp.zeros((lhs.shape[1], w_ref.shape[2]), jnp.float32)
        for j in range(room):
            total = total + jnp.dot(
                lhs[lists_ref[size + q * room + j]],
                w_ref[lists_ref[q * room + j]],
                preferred_element_type=jnp.float32,
            )
        for c in range(n_view):
            back_ref[c, q] = total[c * pc : (c + 1) * pc].astype(jnp.bfloat16)
        return carry

    order = sorted(range(1, n_view), key=lambda k: -min(k, n_view - k))
    rest = pl.ds(1, n_view - 1)
    for g in range(groups):
        lax.fori_loop(per_group * g, per_group * (g + 1), project, 0)
        if g == 0:
            pl.semaphore_wait(barrier, n_view - 1)
        piece = pl.ds(per_group * g, per_group)
        for k in order:
            push(back_ref.at[peer_of(k), piece], rback.at[k, piece], send_sem, recv_sem.at[g], k)
    first = pl.multiple_of(me * pc, pc)
    v = vol_ref[pl.ds(first, pc)]
    before = vol_ref[jnp.maximum(first - 1, 0)]
    before = jnp.where(me > 0, before, 0.0)
    after = vol_ref[jnp.minimum(first + pc, planes - 1)]
    after = jnp.where(me < n_view - 1, after, 0.0)
    row = lax.broadcasted_iota(jnp.int32, (pc, rows, cols), 1)
    col = lax.broadcasted_iota(jnp.int32, (pc, rows, cols), 2)
    above = jnp.where(tile > 0, halo_ref[0], 0.0)[:, None, :]
    below = jnp.where(tile < n_tile - 1, halo_ref[1], 0.0)[:, None, :]

    def term(other):
        return jnp.clip(v - other, -HUBER_DELTA, HUBER_DELTA)

    penalty = term(jnp.concatenate([before[None], v[: pc - 1]], axis=0))
    penalty += term(jnp.concatenate([v[1:], after[None]], axis=0))
    penalty += term(jnp.where(row == 0, above, pltpu.roll(v, 1, 1)))
    penalty += term(jnp.where(row == rows - 1, below, pltpu.roll(v, rows - 1, 1)))
    penalty += term(jnp.where(col == 0, 0.0, pltpu.roll(v, 1, 2)))
    penalty += term(jnp.where(col == cols - 1, 0.0, pltpu.roll(v, cols - 1, 2)))
    scale = v / (1.0 + penalty)

    sens = rsens[0]
    for k in range(1, n_view):
        sens = sens + rsens[k]

    def finish(g):
        landed = rback.at[rest, pl.ds(per_group * g, per_group)]
        pltpu.make_async_copy(landed, landed, recv_sem.at[g]).wait()
        parts = []
        for j in range(per_group):
            q = per_group * g + j
            total = back_ref[me, q].astype(jnp.float32)
            for k in range(1, n_view):
                total = total + rback[k, q].astype(jnp.float32)
            parts.append(total / sens[q : q + 1])
        for h in range(rows // per_group):
            lanes = slice(LANES * h, LANES * (h + 1))
            for i, out in enumerate(swap_chunks([x[:, lanes] for x in parts], seg_cols)):
                natural[g, pl.ds(per_group * h + i, pc, stride=rows), :] = out
        lanes = slice(LANES * g, LANES * (g + 1))
        out_ref[pl.ds(first, pc), :, lanes] = scale[:, :, lanes] * natural[g].reshape(
            pc, rows, LANES
        )

    def piece_of(owner, g):
        return out_ref.at[pl.ds(pl.multiple_of(owner * pc, pc), pc), :, LANES * g : LANES * (g + 1)]

    far = n_view // 2
    relays = {}

    def relay(side, hop, g):
        owner = lax.rem(me + (n_view - hop if side == 0 else hop), n_view)
        piece = piece_of(owner, g)
        relays[side, hop, g] = push(
            piece, piece, gsend_sem, grecv_sem.at[side, hop, g],
            1 if side == 0 else n_view - 1,
        )

    def reach(side, g):
        return far if (side == 0) == (g < groups // 2) else n_view - 1 - far

    for g in range(groups):
        finish(g)
        for side in (0, 1):
            if reach(side, g) > 0:
                relay(side, 0, g)
    for hop in range(1, far + 1):
        for g in range(groups):
            for side in (0, 1):
                if hop <= reach(side, g):
                    relays[side, hop - 1, g].wait_recv()
                    if hop < reach(side, g):
                        relay(side, hop, g)
    for sent, sem in (
        (rback.at[rest], send_sem),
        (out_ref.at[pl.ds(0, planes - pc)], gsend_sem),
    ):
        pltpu.make_async_copy(sent, sent, sem).wait()


def per_device(volume, weights, measured, crossings, counts):
    n_tile = lax.axis_size("tile")
    n_view = lax.axis_size("view")
    planes, rows, cols = volume.shape
    views, slots, bins, seg_pixels = weights.shape[1:]
    seg_cols = seg_pixels // rows
    seg_total = cols // seg_cols
    blocks_view = n_tile // views
    pc = planes // n_view
    half = bins // 2
    total = views * blocks_view
    dims = (planes, rows, cols, seg_cols, views, slots, blocks_view, bins, pc)
    f32, bf16 = jnp.float32, jnp.bfloat16
    vmem = pl.BlockSpec(memory_space=pltpu.VMEM)
    smem = pl.BlockSpec(memory_space=pltpu.SMEM)
    dma = pltpu.SemaphoreType.DMA
    local = pltpu.CompilerParams(vmem_limit_bytes=VMEM_LIMIT)

    def remote(number):
        return pltpu.CompilerParams(
            vmem_limit_bytes=VMEM_LIMIT, collective_id=number, has_side_effects=True
        )

    cross = crossings[0].transpose(0, 2, 1).reshape(views * 2 * slots)
    count = counts[0]
    slot_weights = weights.reshape(views * slots, bins, seg_pixels)
    dense, edges, lists, sens = pl.pallas_call(
        functools.partial(forward_kernel, dims),
        out_shape=(
            jax.ShapeDtypeStruct((total, half, LANES), bf16),
            jax.ShapeDtypeStruct((2, pc, cols), f32),
            jax.ShapeDtypeStruct((2 * (seg_total * 2 * views + LANES),), jnp.int32),
            jax.ShapeDtypeStruct((seg_total, seg_pixels), f32),
        ),
        in_specs=[smem, smem, vmem, vmem],
        out_specs=(vmem, vmem, smem, vmem),
        scratch_shapes=[
            pltpu.VMEM((cols // LANES, planes * rows, LANES), f32),
            pltpu.VMEM((seg_total, 2 * planes, seg_pixels), bf16),
            pltpu.VMEM((total + 1, half, LANES), f32),
            pltpu.SMEM((seg_total,), jnp.int32),
            pltpu.VMEM((seg_total + 1, 8, seg_pixels), f32),
        ],
        compiler_params=local,
        name="forward",
    )(cross, count, volume.reshape(planes * rows, cols), slot_weights)
    ratios, halo, rsens = pl.pallas_call(
        functools.partial(exchange_kernel, n_tile, n_view),
        out_shape=(
            jax.ShapeDtypeStruct((total, half, LANES), bf16),
            jax.ShapeDtypeStruct((2, pc, cols), f32),
            jax.ShapeDtypeStruct((n_view, seg_total, seg_pixels), f32),
        ),
        in_specs=[vmem, vmem, vmem, vmem],
        out_specs=(vmem, vmem, vmem),
        scratch_shapes=[
            pltpu.VMEM((n_tile, half, LANES), bf16),
            dma, dma, dma, dma, dma, dma, dma((2,)), dma((2,)),
        ],
        compiler_params=remote(1),
        name="exchange",
    )(dense, measured[0, 0, 0].T, edges, sens)
    return pl.pallas_call(
        functools.partial(update_kernel, (n_tile, n_view, seg_cols, 2 * views)),
        out_shape=jax.ShapeDtypeStruct((planes, rows, cols), f32),
        in_specs=[smem, vmem, vmem, vmem, vmem, vmem],
        out_specs=vmem,
        scratch_shapes=[
            pltpu.VMEM((total + 1, planes, bins), bf16),
            pltpu.VMEM((n_view, seg_total, pc, seg_pixels), bf16),
            pltpu.VMEM((n_view, seg_total, pc, seg_pixels), bf16),
            pltpu.VMEM((cols // LANES, pc * rows, LANES), f32),
        ]
        + [dma, dma, dma((cols // LANES,)), dma((2, n_view // 2, cols // LANES))],
        compiler_params=remote(2),
        name="update",
    )(lists, ratios, slot_weights, volume, halo, rsens)


def solution(mesh):
    in_specs = (
        P(None, "tile", None),
        P("tile", "view", None, None, None),
        P("tile", "view", None, None, None),
        P("tile", "view", None, None),
        P("tile", "view"),
    )
    out_specs = P(None, "tile", None)
    return jax.shard_map(
        per_device, mesh=mesh, in_specs=in_specs, out_specs=out_specs, check_vma=False
    )
```
